32 devices in a mesh: lat: 4 (over y, x), lon: 8 (over z, core).
Axes of the slice: x: 2, y: 2, z: 4, core: 2. Of those that a mesh axis runs over, the one named last changes fastest.
Arguments:
- departures: bfloat16 [65536, 256], P(('lat', 'lon')), may hold values from -6 to 6
- footprint: int32 [65536, 4], P(('lat', 'lon')), may hold values from 0 to 131071, as said below
- channel_map: bfloat16 [256, 128], replicated, may hold values from -0.375 to 0.375
- adjoint_in: float32 [128, 128, 1024], P(None, 'lat', 'lon'), may hold values from -6 to 6
- wind_lon: float32 [128, 128, 1024], P(None, 'lat', 'lon'), may hold values from -0.4 to 0.4
- wind_lat: float32 [128, 128, 1024], P(None, 'lat', 'lon'), may hold values from -0.4 to 0.4
Outputs:
- adjoint_out: float32 [128, 128, 1024], P(None, 'lat', 'lon')
The draws below stay inside these ranges and needn't reach their ends.
Inputs may be any that keep to these rules, and one draw needn't show every extreme that they name: `footprint`: the 4 columns of an observation form a 2 by 2 block of neighbouring columns that lie in one device's block of 32 x 128 columns (wrapping inside that block). The observations of one holder device fall into at most 128 per owner device, and in every holder's rows some owner device receives exactly 128.
All inputs are finite; a program needn't handle non-finite values.
Results may differ from the reference program's by a relative error of at most 0.0015.
Values may be sent and summed in bfloat16 or wider, within the bound.
A program may use at most 64 MiB of HBM per device.

```python
import jax
import jax.numpy as jnp
from jax import lax

CH = 256
LEV = 128
FOOT = 4
STEPS = 2
CLAT = 32
CLON = 128
OBS_DEV = 2048
CAP = 128
NLAT = 128
NLON = 1024
OBS = 65536
N_LON = 8
DEVICES = 32


def draw_footprint(key, part):
    slot_count = DEVICES * CAP
    key_noise = jax.random.fold_in(key, 11)
    key_weight = jax.random.fold_in(key, 12)
    key_hot = jax.random.fold_in(key, 13)
    key_shuffle = jax.random.fold_in(key, 14)
    key_row = jax.random.fold_in(key, 15)
    key_col = jax.random.fold_in(key, 16)
    slot_noise = jax.random.randint(key_noise, (DEVICES, slot_count), 0, 2 ** 15)
    owner_weight = jax.random.randint(key_weight, (DEVICES,), 0, 4)
    hot_owner = jax.random.randint(key_hot, (DEVICES, 1), 0, DEVICES)
    slot_owner = jnp.arange(slot_count, dtype=jnp.int32) // CAP
    slot_score = slot_noise + owner_weight[slot_owner][None, :] * 2 ** 13
    slot_score = slot_score + jnp.where(slot_owner[None, :] == hot_owner, 2 ** 17, 0)
    slot_score = slot_score * 4096 + jnp.arange(slot_count, dtype=jnp.int32)[None, :]
    chosen = lax.top_k(slot_score, OBS_DEV)[1]
    shuffle_score = jax.random.randint(key_shuffle, (DEVICES, OBS_DEV), 0, 2 ** 18) * 4096
    shuffle_score = shuffle_score + jnp.arange(OBS_DEV, dtype=jnp.int32)[None, :]
    order = jnp.argsort(shuffle_score, axis=1, stable=True)
    chosen = jnp.take_along_axis(chosen, order, axis=1)
    owner_index = chosen // CAP
    owner_lat = owner_index // N_LON
    owner_lon = owner_index % N_LON
    row_base = jax.random.randint(key_row, (DEVICES, OBS_DEV), 0, CLAT)
    col_base = jax.random.randint(key_col, (DEVICES, OBS_DEV), 0, CLON)
    pieces = []
    for row_step, col_step in ((0, 0), (0, 1), (1, 0), (1, 1)):
        grid_lat = owner_lat * CLAT + (row_base + row_step) % CLAT
        grid_lon = owner_lon * CLON + (col_base + col_step) % CLON
        pieces.append(grid_lat * NLON + grid_lon)
    return jnp.stack(pieces, -1).reshape(OBS, FOOT).astype(jnp.int32)


def block_levels(stream_key, extent, cuts, least, high):
    loudness, own = 1.0, jax.random.fold_in(stream_key, 6)
    for dim, shards_of in cuts:
        heights = jnp.exp(jax.random.uniform(jax.random.fold_in(own, dim), (shards_of,), jnp.float32, least / len(cuts), high / len(cuts)))
        loudness = loudness * jnp.repeat(heights, extent[dim] // shards_of).reshape([-1 if axis == dim else 1 for axis in range(len(extent))])
    return loudness


def noise(stream_key, extent, width, limit, cuts=(), held_as=jnp.bfloat16):
    drawn = jax.random.normal(stream_key, extent, jnp.float32) * width
    if len(cuts) > 0:
        drawn = block_levels(stream_key, extent, cuts, -0.22, 0.18) * drawn
    return jnp.clip(drawn, min=-limit, max=limit).astype(held_as)


def setup_inputs(seed: int = 0) -> dict:
    streams_of = jax.random.split(jax.random.key(seed), 7)
    departures = noise(streams_of[0], (OBS, CH), 1.0, 6.0, ((0, 32),))
    footprint = draw_footprint(jax.random.fold_in(streams_of[6], 71), 0)
    channel_map = noise(streams_of[2], (CH, LEV), CH ** -0.5, 0.375)
    adjoint_in = noise(streams_of[3], (LEV, NLAT, NLON), 1.0, 6.0, ((1, 4), (2, 8)), jnp.float32)
    wind_lon = jnp.clip(jax.random.uniform(streams_of[4], (LEV, NLAT, NLON), jnp.float32, -0.4, 0.4) * block_levels(streams_of[4], (LEV, NLAT, NLON), ((1, 4), (2, 8)), -0.4, 0.0), -0.4, 0.4)
    wind_lat = jnp.clip(jax.random.uniform(streams_of[5], (LEV, NLAT, NLON), jnp.float32, -0.4, 0.4) * block_levels(streams_of[5], (LEV, NLAT, NLON), ((1, 4), (2, 8)), -0.4, 0.0), -0.4, 0.4)
    return dict(departures=departures, footprint=footprint, channel_map=channel_map, adjoint_in=adjoint_in, wind_lon=wind_lon, wind_lat=wind_lat)


diffusion_rate = 0.2


def deposit_profiles(profiles, columns, column_count):
    values = profiles.astype(jnp.float32)
    deposit = jnp.zeros((column_count, values.shape[1]), jnp.float32)
    for corner in range(FOOT):
        deposit = deposit + jax.ops.segment_sum(values, columns[:, corner], num_segments=column_count)
    return deposit * 0.25


def lon_sides(field):
    return jnp.roll(field, -1, 2), jnp.roll(field, 1, 2)


def lat_sides(field):
    padded = jnp.pad(field, ((0, 0), (1, 1), (0, 0)))
    return padded[:, 2:, :], padded[:, :-2, :]


def adjoint_step(adjoint_state, wind_lon, wind_lat):
    east_side, west_side = lon_sides(adjoint_state)
    north_side, south_side = lat_sides(adjoint_state)
    east_flux, west_flux = lon_sides(wind_lon * adjoint_state)
    north_flux, south_flux = lat_sides(wind_lat * adjoint_state)
    laplace = east_side + west_side + north_side + south_side - 4.0 * adjoint_state
    return adjoint_state + diffusion_rate * laplace + 0.5 * (east_flux - west_flux) + 0.5 * (north_flux - south_flux)


def reference(departures, footprint, channel_map, adjoint_in, wind_lon, wind_lat):
    profiles = jnp.dot(departures, channel_map, preferred_element_type=jnp.float32).astype(jnp.bfloat16)
    deposit = deposit_profiles(profiles, footprint, NLAT * NLON)
    adjoint_state = adjoint_in + deposit.T.reshape(LEV, NLAT, NLON)
    for advect_step in range(STEPS):
        adjoint_state = adjoint_step(adjoint_state, wind_lon, wind_lat)
    return adjoint_state
```

```python
import functools

import jax
import jax.numpy as jnp
from jax import lax
from jax.experimental import pallas as pl
from jax.experimental.pallas import tpu as pltpu
from jax.sharding import PartitionSpec as P

STEPS = 2
RATE = 0.2
LANES = 128
META = 16
PART = 16
MESH = pl.DeviceIdType.MESH


def log2(size):
    assert size & (size - 1) == 0
    return size.bit_length() - 1


def nt_dot(a, b):
    return lax.dot_general(a, b, (((1,), (1,)), ((), ())), preferred_element_type=jnp.float32)


def xor(n, v, mask):
    total = 0
    for bit in range(log2(n)):
        here, other = v // 2 ** bit % 2, mask // 2 ** bit % 2
        total = total + 2 ** bit * (here + other - 2 * here * other)
    return total


def chunks_of(levels):
    assert levels % (4 * PART) == 0
    return [(q * (levels // 4), levels // 4) for q in range(4)]


def kernel(
    n_lat, n_lon, foot, dep_hbm, cmap, adj_hbm, wlon_hbm, wlat_hbm, out,
    dep, prof, tag, send, recv, meta_send, meta_recv, cell_hot, row_hot,
    state, later, wlon, wlat, edge_out, edge_in,
    load_sem, send_sem, recv_sem, meta_send_sem, meta_recv_sem, edge_send_sem, edge_recv_sem,
):
    lat, lon = lax.axis_index("lat"), lax.axis_index("lon")
    n_dev = n_lat * n_lon
    rows, levels, cols = state.shape
    obs = dep.shape[0]
    slots = recv.shape[2]
    depth = n_lat * slots
    chunks = chunks_of(levels)

    pltpu.make_async_copy(dep_hbm, dep, load_sem.at[3]).start()

    barrier = pltpu.get_barrier_semaphore()

    def greet(i, carry):
        pl.semaphore_signal(
            barrier, inc=1,
            device_id=((lat + i // n_lon) % n_lat, (lon + i % n_lon) % n_lon),
            device_id_type=MESH,
        )
        return carry

    lax.fori_loop(1, n_dev, greet, 0)

    def load(r, carry):
        pltpu.make_async_copy(adj_hbm.at[:, r, :], state.at[r], load_sem.at[0]).start()
        pltpu.make_async_copy(wlon_hbm.at[:, r, :], wlon.at[r], load_sem.at[1]).start()
        pltpu.make_async_copy(wlat_hbm.at[:, r, :], wlat.at[r], load_sem.at[2]).start()
        return carry

    shift_grid, shift_row, shift_col = log2(n_lon * cols), log2(rows), log2(cols)
    cells = foot[...]
    grid_row = lax.shift_right_logical(cells, shift_grid)
    grid_col = cells & (n_lon * cols - 1)
    owner = (
        lax.shift_right_logical(grid_row[0:1], shift_row) * n_lon
        + lax.shift_right_logical(grid_col[0:1], shift_col)
    )
    in_row = grid_row & (rows - 1)
    in_col = grid_col & (cols - 1)

    def base(cell):
        low = jnp.minimum(jnp.minimum(cell[0:1], cell[1:2]), jnp.minimum(cell[2:3], cell[3:4]))
        high = jnp.maximum(jnp.maximum(cell[0:1], cell[1:2]), jnp.maximum(cell[2:3], cell[3:4]))
        return jnp.where(high - low == 1, low, high)

    base_row, base_col = base(in_row), base(in_col)
    chunk = 256
    upper = jnp.where(
        lax.broadcasted_iota(jnp.int32, (chunk, chunk), 0)
        <= lax.broadcasted_iota(jnp.int32, (chunk, chunk), 1),
        1.0, 0.0,
    ).astype(jnp.bfloat16)
    owners = lax.broadcasted_iota(jnp.int32, (n_dev, chunk), 0)
    seen = jnp.zeros((n_dev, 1), jnp.float32)
    for start in range(0, obs, chunk):
        hot = jnp.where(owners == owner[:, start:start + chunk], 1.0, 0.0)
        count = jnp.dot(hot.astype(jnp.bfloat16), upper, preferred_element_type=jnp.float32) + seen
        place = jnp.sum(hot * count, axis=0, keepdims=True) - 1.0
        seen = count[:, chunk - 1:chunk]
        tag[0:1, start:start + chunk] = place.astype(jnp.int32)
    tag[1:2, :] = owner

    pltpu.make_async_copy(dep_hbm, dep, load_sem.at[3]).wait()
    lax.fori_loop(0, rows, load, 0)
    prof[0:levels, :] = lax.dot_general(
        cmap[...], dep[...], (((0,), (1,)), ((), ())), preferred_element_type=jnp.float32
    ).astype(jnp.bfloat16)
    which = lax.broadcasted_iota(jnp.int32, (META, obs), 0)
    prof[levels:levels + META, :] = jnp.where(
        which == 0, base_row, jnp.where(which == 1, base_col, 0)
    ).astype(jnp.float32).astype(jnp.bfloat16)

    @pl.when(lat == 0)
    def _():
        edge_in[:, 3] = jnp.zeros_like(edge_in[:, 3])

    @pl.when(lat == n_lat - 1)
    def _():
        edge_in[:, 2] = jnp.zeros_like(edge_in[:, 2])

    pl.semaphore_wait(barrier, n_dev - 1)

    own = n_lon - 1

    def target(k, a):
        return xor(n_lat, lat, a), xor(n_lon, lon, n_lon - 1 - k)

    def block_copy(c, k, a):
        i, (first, size) = k * n_lat + a, chunks[c]
        at = pl.ds(first, size)
        return pltpu.make_async_remote_copy(
            src_ref=send.at[i, at], dst_ref=recv.at[i, at],
            send_sem=send_sem.at[c], recv_sem=recv_sem.at[c, k],
            device_id=target(k, a), device_id_type=MESH,
        )

    def meta_copy(k, a):
        i = k * n_lat + a
        return pltpu.make_async_remote_copy(
            src_ref=meta_send.at[i], dst_ref=meta_recv.at[i],
            send_sem=meta_send_sem, recv_sem=meta_recv_sem.at[k],
            device_id=target(k, a), device_id_type=MESH,
        )

    def route(k, carry):
        place, owner = tag[0:1, :], tag[1:2, :]
        slot = lax.broadcasted_iota(jnp.int32, (slots, obs), 0)
        hots = []
        for a in range(n_lat):
            to_lat, to_lon = target(k, a)
            wanted = jnp.where(owner == to_lat * n_lon + to_lon, place, -1)
            hots.append(jnp.where(slot == wanted, 1.0, 0.0).astype(jnp.bfloat16))
        blocks = nt_dot(prof[...], jnp.concatenate(hots, axis=0))
        meta = (blocks[levels:levels + 1] * cols + blocks[levels + 1:levels + 2]).astype(jnp.int32)
        blocks = blocks[0:levels].astype(jnp.bfloat16)
        for a in range(n_lat):
            i = k * n_lat + a
            at = slice(a * slots, (a + 1) * slots)

            def away():
                send[i] = blocks[:, at]
                meta_send[i] = meta[:, at]
                block_copy(0, k, a).start()
                meta_copy(k, a).start()

            if a == 0:
                @pl.when(k == own)
                def _():
                    recv[i] = blocks[:, at]
                    meta_recv[i] = meta[:, at]

                pl.when(k != own)(away)
            else:
                away()
        return carry

    lax.fori_loop(0, n_lon, route, 0)

    def ship(c):
        def some(k, carry):
            for a in range(n_lat):
                if a == 0:
                    @pl.when(k != own)
                    def _():
                        block_copy(c, k, 0).start()
                else:
                    block_copy(c, k, a).start()
            return carry

        lax.fori_loop(0, n_lon, some, 0)

    def await_group(k, ref, sem):
        @pl.when(k != own)
        def _():
            here = ref(pl.ds(k * n_lat, n_lat))
            pltpu.make_async_copy(here, here, sem).wait()

        @pl.when(k == own)
        def _():
            here = ref(pl.ds(k * n_lat + 1, n_lat - 1))
            pltpu.make_async_copy(here, here, sem).wait()

    def read_meta(k):
        await_group(k, lambda i: meta_recv.at[i], meta_recv_sem.at[k])
        meta = jnp.concatenate([meta_recv[k * n_lat + a] for a in range(n_lat)], axis=1)
        at_row, at_col = lax.shift_right_logical(meta, shift_col), meta & (cols - 1)
        cell = lax.broadcasted_iota(jnp.int32, (2 * cols, depth), 0)
        first = at_row % 2 * cols
        cell_hot[k] = jnp.where(
            (cell == first + at_col) | (cell == first + ((at_col + 1) & (cols - 1))), 0.25, 0.0
        ).astype(jnp.bfloat16)
        pair = lax.shift_right_logical(at_row, 1)
        for p in range(rows // 2):
            hot = jnp.where(pair == p, 1.0, 0.0)
            row_hot[k, p] = jnp.broadcast_to(hot, (16, depth)).astype(jnp.bfloat16)

    def deposit(c):
        start, size = chunks[c]
        at = pl.ds(start, size)
        tile = min(rows // 2, max(1, 512 // size))

        def group(k, carry):
            if c == 0:
                read_meta(k)
            await_group(k, lambda i: recv.at[i, at], recv_sem.at[c, k])
            got = jnp.concatenate([recv[k * n_lat + a, at, :] for a in range(n_lat)], axis=1)
            stacked = got.reshape(size // 16, 16, depth)

            def rows_of(t, carry):
                lhs = []
                for j in range(tile):
                    lhs.append((stacked * row_hot[k, t * tile + j][None]).reshape(size, depth))
                found = nt_dot(jnp.concatenate(lhs, axis=0), cell_hot[k])
                for j in range(tile):
                    r = 2 * (t * tile + j)
                    here = found[j * size:(j + 1) * size]
                    later[r, at, :] = later[r, at, :] + here[:, 0:cols]
                    later[r + 1, at, :] = later[r + 1, at, :] + here[:, cols:2 * cols]
                return carry

            lax.fori_loop(0, rows // 2 // tile, rows_of, 0)
            return carry

        lax.fori_loop(0, n_lon, group, 0)

    assert 2 * rows <= cols and rows % 4 == 0
    lane = lax.broadcasted_iota(jnp.int32, (PART, cols), 1)
    side_half = jnp.where(lane == cols - 1, -0.5, 0.5)
    west, east = (lon + n_lon - 1) % n_lon, (lon + 1) % n_lon
    south, north = (lat + n_lat - 1) % n_lat, (lat + 1) % n_lat
    targets = ((lat, west), (lat, east), (south, lon), (north, lon))

    def edge_copy(step, c, side):
        at = pl.ds(*chunks[c])
        return pltpu.make_async_remote_copy(
            src_ref=edge_out.at[step, max(side, 1), at], dst_ref=edge_in.at[step, side, at],
            send_sem=edge_send_sem.at[step, c, side], recv_sem=edge_recv_sem.at[step, c, side],
            device_id=targets[side], device_id_type=MESH,
        )

    def send_edges(step, c):
        edge_copy(step, c, 0).start()
        edge_copy(step, c, 1).start()

        @pl.when(lat > 0)
        def _():
            edge_copy(step, c, 2).start()

        @pl.when(lat < n_lat - 1)
        def _():
            edge_copy(step, c, 3).start()

    def await_edges(step, c):
        edge_copy(step, c, 0).wait()
        edge_copy(step, c, 1).wait()

        @pl.when(lat > 0)
        def _():
            edge_copy(step, c, 2).wait_send()
            edge_copy(step, c, 3).wait_recv()

        @pl.when(lat < n_lat - 1)
        def _():
            edge_copy(step, c, 3).wait_send()
            edge_copy(step, c, 2).wait_recv()

    def split(s, w):
        flux = (0.5 * w) * s
        even = RATE * s
        return even + flux, even - flux

    def pack_row(packed, r, s, w):
        side = (RATE + side_half * w) * s
        if r > 0:
            side = pltpu.roll(side, 2 * r, 1)
        return jnp.where((lane == 2 * r) | (lane == (2 * r - 1) % cols), side, packed)

    def pack_edge(step, at, r, s):
        if r == 0:
            edge_out[step, 2, at, :] = split(s, wlat[r, at, :])[0].astype(jnp.bfloat16)
        if r == rows - 1:
            edge_out[step, 3, at, :] = split(s, wlat[r, at, :])[1].astype(jnp.bfloat16)

    def parts(c, work):
        start, size = chunks[c]

        def some(q, carry):
            work(pl.ds(pl.multiple_of(start + q * PART, PART), PART))
            return carry

        lax.fori_loop(0, size // PART, some, 0)

    def combine(c):
        def work(at):
            packed = jnp.zeros((PART, cols), jnp.float32)
            below = later[rows - 1, at, :]
            for r in range(rows):
                here = later[r, at, :]
                s = state[r, at, :] + (here + below)
                state[r, at, :] = s
                packed = pack_row(packed, r, s, wlon[r, at, :])
                pack_edge(0, at, r, s)
                below = here
            edge_out[0, 1, at, :] = packed.astype(jnp.bfloat16)

        parts(c, work)
        send_edges(0, c)

    def advance(step, c):
        last = step == STEPS - 1
        src = state if step % 2 == 0 else later
        dst = out if last else later if step % 2 == 0 else state

        def work(at):
            both = jnp.where(
                lane % 2 == 0,
                edge_in[step, 0, at, :].astype(jnp.float32),
                pltpu.roll(edge_in[step, 1, at, :].astype(jnp.float32), 2, 1),
            )
            packed = jnp.zeros((PART, cols), jnp.float32)
            centre = None
            below = edge_in[step, 3, at, :].astype(jnp.float32)
            for r in range(rows + 1):
                if r < rows:
                    s = src[r, at, :]
                    plus, minus = split(s, wlon[r, at, :])
                    moved = pltpu.roll(both, (cols - 1 - 2 * r) % cols, 1)
                    across = (
                        (1.0 - 4.0 * RATE) * s
                        + jnp.where(lane == cols - 1, moved, pltpu.roll(plus, cols - 1, 1))
                        + jnp.where(lane == 0, moved, pltpu.roll(minus, 1, 1))
                    )
                    above, here = split(s, wlat[r, at, :])
                else:
                    above = edge_in[step, 2, at, :].astype(jnp.float32)
                if r > 0:
                    total = centre + above
                    dst[r - 1, at, :] = total
                    if not last:
                        packed = pack_row(packed, r - 1, total, wlon[r - 1, at, :])
                        pack_edge(step + 1, at, r - 1, total)
                if r < rows:
                    centre = across + below
                    below = here
            if not last:
                edge_out[step + 1, 1, at, :] = packed.astype(jnp.bfloat16)

        await_edges(step, c)
        parts(c, work)
        if not last:
            send_edges(step + 1, c)

    ship(1)
    later[...] = jnp.zeros_like(later)
    deposit(0)
    for which, buf in enumerate((state, wlon, wlat)):
        pltpu.make_async_copy(buf, buf, load_sem.at[which]).wait()
    combine(0)
    ship(2)
    deposit(1)
    combine(1)
    ship(3)
    deposit(2)
    combine(2)
    advance(0, 0)
    deposit(3)
    combine(3)
    advance(0, 1)
    advance(1, 0)
    advance(0, 2)
    advance(1, 1)
    advance(0, 3)
    advance(1, 2)
    advance(1, 3)

    for c in range(len(chunks)):
        sent = send.at[pl.ds(0, n_dev - 1), pl.ds(*chunks[c])]
        pltpu.make_async_copy(sent, sent, send_sem.at[c]).wait()
    sent = meta_send.at[pl.ds(0, n_dev - 1)]
    pltpu.make_async_copy(sent, sent, meta_send_sem).wait()


def write_out(x, out, sem):
    def put(r, carry):
        pltpu.make_async_copy(x.at[r], out.at[:, r, :], sem).start()
        return carry

    lax.fori_loop(0, x.shape[0], put, 0)
    pltpu.make_async_copy(x, x, sem).wait()


def local(departures, footprint, channel_map, adjoint_in, wind_lon, wind_lat):
    n_lat, n_lon = lax.axis_size("lat"), lax.axis_size("lon")
    n_dev = n_lat * n_lon
    levels, rows, cols = adjoint_in.shape
    obs = departures.shape[0]
    capacity = 2 * obs // n_dev
    slots = -(-capacity // LANES) * LANES
    depth = n_lat * slots
    n_chunks = len(chunks_of(levels))
    block = pltpu.VMEM((n_dev, levels, slots), jnp.bfloat16)
    meta = pltpu.VMEM((n_dev, 1, slots), jnp.int32)
    field = pltpu.VMEM((rows, levels, cols), jnp.float32)
    edges = pltpu.VMEM((STEPS, 4, levels, cols), jnp.bfloat16)
    vmem, anywhere = pl.BlockSpec(memory_space=pltpu.VMEM), pl.BlockSpec(memory_space=pl.ANY)
    hbm = pl.BlockSpec(memory_space=pltpu.HBM)
    result = pl.pallas_call(
        functools.partial(kernel, n_lat, n_lon),
        out_shape=pltpu.VMEM((rows, levels, cols), jnp.float32),
        in_specs=[vmem, hbm, vmem] + [hbm] * 3,
        out_specs=vmem,
        scratch_shapes=[
            pltpu.VMEM(departures.shape, jnp.bfloat16),
            pltpu.VMEM((levels + META, obs), jnp.bfloat16),
            pltpu.VMEM((8, obs), jnp.int32),
            block, block, meta, meta,
            pltpu.VMEM((n_lon, 2 * cols, depth), jnp.bfloat16),
            pltpu.VMEM((n_lon, rows // 2, 16, depth), jnp.bfloat16),
            field, field, field, field,
            edges, edges,
            pltpu.SemaphoreType.DMA((4,)),
            pltpu.SemaphoreType.DMA((n_chunks,)),
            pltpu.SemaphoreType.DMA((n_chunks, n_lon)),
            pltpu.SemaphoreType.DMA,
            pltpu.SemaphoreType.DMA((n_lon,)),
            pltpu.SemaphoreType.DMA((STEPS, n_chunks, 4)),
            pltpu.SemaphoreType.DMA((STEPS, n_chunks, 4)),
        ],
        compiler_params=pltpu.CompilerParams(
            collective_id=0, has_side_effects=True, vmem_limit_bytes=52 << 20
        ),
        name="assimilate",
    )(footprint.T, departures, channel_map, adjoint_in, wind_lon, wind_lat)
    return pl.pallas_call(
        write_out,
        out_shape=jax.ShapeDtypeStruct(adjoint_in.shape, jnp.float32),
        in_specs=[vmem],
        out_specs=hbm,
        scratch_shapes=[pltpu.SemaphoreType.DMA],
        compiler_params=pltpu.CompilerParams(vmem_limit_bytes=8 << 20),
        name="write_out",
    )(result)


def solution(mesh):
    in_specs = (
        P(("lat", "lon"), None),
        P(("lat", "lon"), None),
        P(),
        P(None, "lat", "lon"),
        P(None, "lat", "lon"),
        P(None, "lat", "lon"),
    )
    out_specs = P(None, "lat", "lon")
    return jax.shard_map(local, mesh=mesh, in_specs=in_specs, out_specs=out_specs, check_vma=False)
```

```python
import functools

import jax
import jax.numpy as jnp
from jax import lax
from jax.experimental import pallas as pl
from jax.experimental.pallas import tpu as pltpu
from jax.sharding import PartitionSpec as P

STEPS = 2
RATE = 0.2
LANES = 128
META = 16
PART = 16
MESH = pl.DeviceIdType.MESH


def log2(size):
    assert size & (size - 1) == 0
    return size.bit_length() - 1


def nt_dot(a, b):
    return lax.dot_general(a, b, (((1,), (1,)), ((), ())), preferred_element_type=jnp.float32)


def nn_dot(a, b):
    return lax.dot_general(a, b, (((1,), (0,)), ((), ())), preferred_element_type=jnp.float32)


def xor(n, v, mask):
    total = 0
    for bit in range(log2(n)):
        here, other = v // 2 ** bit % 2, mask // 2 ** bit % 2
        total = total + 2 ** bit * (here + other - 2 * here * other)
    return total


def chunks_of(levels):
    assert levels % (4 * PART) == 0
    return [(q * (levels // 4), levels // 4) for q in range(4)]


def kernel(
    n_lat, n_lon, foot, dep_hbm, cmap, adj_hbm, wlon_hbm, wlat_hbm, out,
    dep, prof, key, send, recv, meta_send, meta_recv, cell_hot, row_hot,
    state, later, wlon, wlat, edge_out, edge_in,
    load_sem, send_sem, recv_sem, meta_send_sem, meta_recv_sem, edge_send_sem, edge_recv_sem,
):
    lat, lon = lax.axis_index("lat"), lax.axis_index("lon")
    n_dev = n_lat * n_lon
    rows, levels, cols = state.shape
    obs = dep.shape[0]
    slots = recv.shape[2]
    depth = n_lat * slots
    chunks = chunks_of(levels)

    pltpu.make_async_copy(dep_hbm, dep, load_sem.at[3]).start()

    barrier = pltpu.get_barrier_semaphore()

    def greet(i, carry):
        pl.semaphore_signal(
            barrier, inc=1,
            device_id=((lat + i // n_lon) % n_lat, (lon + i % n_lon) % n_lon),
            device_id_type=MESH,
        )
        return carry

    lax.fori_loop(1, n_dev, greet, 0)

    def load(r, carry):
        pltpu.make_async_copy(adj_hbm.at[:, r, :], state.at[r], load_sem.at[0]).start()
        pltpu.make_async_copy(wlon_hbm.at[:, r, :], wlon.at[r], load_sem.at[1]).start()
        pltpu.make_async_copy(wlat_hbm.at[:, r, :], wlat.at[r], load_sem.at[2]).start()
        return carry

    shift_grid, shift_row, shift_col = log2(n_lon * cols), log2(rows), log2(cols)
    cells = foot[...]
    grid_row = lax.shift_right_logical(cells, shift_grid)
    grid_col = cells & (n_lon * cols - 1)
    owner = (
        lax.shift_right_logical(grid_row[0:1], shift_row) * n_lon
        + lax.shift_right_logical(grid_col[0:1], shift_col)
    )
    in_row = grid_row & (rows - 1)
    in_col = grid_col & (cols - 1)

    def base(cell):
        low = jnp.minimum(jnp.minimum(cell[0:1], cell[1:2]), jnp.minimum(cell[2:3], cell[3:4]))
        high = jnp.maximum(jnp.maximum(cell[0:1], cell[1:2]), jnp.maximum(cell[2:3], cell[3:4]))
        return jnp.where(high - low == 1, low, high)

    base_row, base_col = base(in_row), base(in_col)
    chunk = 256
    upper = jnp.where(
        lax.broadcasted_iota(jnp.int32, (chunk, chunk), 0)
        <= lax.broadcasted_iota(jnp.int32, (chunk, chunk), 1),
        1.0, 0.0,
    ).astype(jnp.bfloat16)
    owners = lax.broadcasted_iota(jnp.int32, (n_dev, chunk), 0)
    seen = jnp.zeros((n_dev, 1), jnp.float32)
    for start in range(0, obs, chunk):
        hot = jnp.where(owners == owner[:, start:start + chunk], 1.0, 0.0)
        count = jnp.dot(hot.astype(jnp.bfloat16), upper, preferred_element_type=jnp.float32) + seen
        place = jnp.sum(hot * count, axis=0, keepdims=True) - 1.0
        seen = count[:, chunk - 1:chunk]
        which = lax.broadcasted_iota(jnp.int32, (16, chunk), 0)
        pair = jnp.where(which == 0, owner[:, start:start + chunk].astype(jnp.float32), place)
        scale = jnp.where(lax.broadcasted_iota(jnp.int32, (16, slots), 0) == 0, slots, 1)
        scale = jnp.where(lax.broadcasted_iota(jnp.int32, (16, slots), 0) < 2, scale, 0)
        key[start:start + chunk, :] = lax.dot_general(
            pair.astype(jnp.bfloat16), scale.astype(jnp.float32).astype(jnp.bfloat16),
            (((0,), (0,)), ((), ())), preferred_element_type=jnp.float32,
        )

    pltpu.make_async_copy(dep_hbm, dep, load_sem.at[3]).wait()
    lax.fori_loop(0, rows, load, 0)
    prof[0:levels, :] = lax.dot_general(
        cmap[...], dep[...], (((0,), (1,)), ((), ())), preferred_element_type=jnp.float32
    ).astype(jnp.bfloat16)
    which = lax.broadcasted_iota(jnp.int32, (META, obs), 0)
    prof[levels:levels + META, :] = jnp.where(
        which == 0, base_row, jnp.where(which == 1, base_col, 0)
    ).astype(jnp.float32).astype(jnp.bfloat16)

    @pl.when(lat == 0)
    def _():
        edge_in[:, 3] = jnp.zeros_like(edge_in[:, 3])

    @pl.when(lat == n_lat - 1)
    def _():
        edge_in[:, 2] = jnp.zeros_like(edge_in[:, 2])

    pl.semaphore_wait(barrier, n_dev - 1)

    own = n_lon - 1

    def target(k, a):
        return xor(n_lat, lat, a), xor(n_lon, lon, n_lon - 1 - k)

    def block_copy(c, k, a):
        i, (first, size) = k * n_lat + a, chunks[c]
        at = pl.ds(first, size)
        return pltpu.make_async_remote_copy(
            src_ref=send.at[i, at], dst_ref=recv.at[i, at],
            send_sem=send_sem.at[c], recv_sem=recv_sem.at[c, k],
            device_id=target(k, a), device_id_type=MESH,
        )

    def meta_copy(k, a):
        i = k * n_lat + a
        return pltpu.make_async_remote_copy(
            src_ref=meta_send.at[i], dst_ref=meta_recv.at[i],
            send_sem=meta_send_sem, recv_sem=meta_recv_sem.at[k],
            device_id=target(k, a), device_id_type=MESH,
        )

    def route(k, carry):
        lane = lax.broadcasted_iota(jnp.int32, (obs, slots), 1)
        hots = []
        for a in range(n_lat):
            to_lat, to_lon = target(k, a)
            wanted = (lane + (to_lat * n_lon + to_lon) * slots).astype(jnp.float32)
            hots.append(jnp.where(key[...] == wanted, 1.0, 0.0).astype(jnp.bfloat16))
        blocks = nn_dot(prof[...], jnp.concatenate(hots, axis=1))
        meta = (blocks[levels:levels + 1] * cols + blocks[levels + 1:levels + 2]).astype(jnp.int32)
        blocks = blocks[0:levels].astype(jnp.bfloat16)
        for a in range(n_lat):
            i = k * n_lat + a
            at = slice(a * slots, (a + 1) * slots)

            def away():
                send[i] = blocks[:, at]
                meta_send[i] = meta[:, at]
                block_copy(0, k, a).start()
                meta_copy(k, a).start()

            if a == 0:
                @pl.when(k == own)
                def _():
                    recv[i] = blocks[:, at]
                    meta_recv[i] = meta[:, at]

                pl.when(k != own)(away)
            else:
                away()
        return carry

    lax.fori_loop(0, n_lon, route, 0)

    def ship(c):
        def some(k, carry):
            for a in range(n_lat):
                if a == 0:
                    @pl.when(k != own)
                    def _():
                        block_copy(c, k, 0).start()
                else:
                    block_copy(c, k, a).start()
            return carry

        lax.fori_loop(0, n_lon, some, 0)

    def await_group(k, ref, sem):
        @pl.when(k != own)
        def _():
            here = ref(pl.ds(k * n_lat, n_lat))
            pltpu.make_async_copy(here, here, sem).wait()

        @pl.when(k == own)
        def _():
            here = ref(pl.ds(k * n_lat + 1, n_lat - 1))
            pltpu.make_async_copy(here, here, sem).wait()

    wide = cell_hot.shape[2]
    groups = wide // depth

    def read_meta(k, carry):
        await_group(k, lambda i: meta_recv.at[i], meta_recv_sem.at[k])
        meta = jnp.concatenate([meta_recv[k * n_lat + a] for a in range(n_lat)], axis=1)
        at_row, at_col = lax.shift_right_logical(meta, shift_col), meta & (cols - 1)
        cell = lax.broadcasted_iota(jnp.int32, (2 * cols, depth), 0)
        first = at_row % 2 * cols
        block, at = k // groups, pl.ds(pl.multiple_of(k % groups * depth, depth), depth)
        cell_hot[block, :, at] = jnp.where(
            (cell == first + at_col) | (cell == first + ((at_col + 1) & (cols - 1))), 0.25, 0.0
        ).astype(jnp.bfloat16)
        pair = lax.shift_right_logical(at_row, 1)
        for p in range(rows // 2):
            hot = jnp.where(pair == p, 1.0, 0.0)
            row_hot[block, p, :, at] = jnp.broadcast_to(hot, (16, depth)).astype(jnp.bfloat16)
        return carry

    def deposit(c):
        start, size = chunks[c]
        at = pl.ds(start, size)
        tile = min(rows // 2, max(1, 512 // size))
        for block in range(n_lon // groups):
            def arrive(k, carry):
                await_group(k, lambda i: recv.at[i, at], recv_sem.at[c, k])
                return carry

            lax.fori_loop(block * groups, (block + 1) * groups, arrive, 0)
            first = block * groups * n_lat
            got = jnp.concatenate([recv[first + i, at, :] for i in range(groups * n_lat)], axis=1)
            stacked = got.reshape(size // 16, 16, wide)
            for t in range(rows // 2 // tile):
                lhs = []
                for j in range(tile):
                    lhs.append((stacked * row_hot[block, t * tile + j][None]).reshape(size, wide))
                found = nt_dot(jnp.concatenate(lhs, axis=0), cell_hot[block])
                for j in range(tile):
                    r = 2 * (t * tile + j)
                    here = found[j * size:(j + 1) * size]
                    low, high = here[:, 0:cols], here[:, cols:2 * cols]
                    if block > 0:
                        low, high = later[r, at, :] + low, later[r + 1, at, :] + high
                    later[r, at, :] = low
                    later[r + 1, at, :] = high

    assert 2 * rows <= cols and rows % 4 == 0
    half = jnp.bfloat16
    lane = lax.broadcasted_iota(jnp.int32, (PART, cols), 1)
    lane_half = lane.astype(jnp.float32).astype(half)
    side_half = jnp.where(lane == cols - 1, -0.5, 0.5)
    at_east, at_west = lane_half == half(cols - 1), lane_half == half(0)
    west, east = (lon + n_lon - 1) % n_lon, (lon + 1) % n_lon
    south, north = (lat + n_lat - 1) % n_lat, (lat + 1) % n_lat
    targets = ((lat, west), (lat, east), (south, lon), (north, lon))

    def edge_copy(step, c, side):
        at = pl.ds(*chunks[c])
        return pltpu.make_async_remote_copy(
            src_ref=edge_out.at[step, max(side, 1), at], dst_ref=edge_in.at[step, side, at],
            send_sem=edge_send_sem.at[step, c, side], recv_sem=edge_recv_sem.at[step, c, side],
            device_id=targets[side], device_id_type=MESH,
        )

    def send_edges(step, c):
        edge_copy(step, c, 0).start()
        edge_copy(step, c, 1).start()

        @pl.when(lat > 0)
        def _():
            edge_copy(step, c, 2).start()

        @pl.when(lat < n_lat - 1)
        def _():
            edge_copy(step, c, 3).start()

    def await_edges(step, c):
        edge_copy(step, c, 0).wait()
        edge_copy(step, c, 1).wait()

        @pl.when(lat > 0)
        def _():
            edge_copy(step, c, 2).wait_send()
            edge_copy(step, c, 3).wait_recv()

        @pl.when(lat < n_lat - 1)
        def _():
            edge_copy(step, c, 3).wait_send()
            edge_copy(step, c, 2).wait_recv()

    def split(s, w):
        flux = (0.5 * w) * s
        even = RATE * s
        return even + flux, even - flux

    def pack_row(packed, r, s, w):
        side = ((RATE + side_half * w) * s).astype(half)
        if r > 0:
            side = pltpu.roll(side, 2 * r, 1)
        here = (lane_half == half(2 * r)) | (lane_half == half((2 * r - 1) % cols))
        return jnp.where(here, side, packed)

    def pack_edge(step, at, r, s):
        if r == 0:
            edge_out[step, 2, at, :] = split(s, wlat[r, at, :])[0].astype(jnp.bfloat16)
        if r == rows - 1:
            edge_out[step, 3, at, :] = split(s, wlat[r, at, :])[1].astype(jnp.bfloat16)

    def parts(c, work):
        start, size = chunks[c]

        def some(q, carry):
            work(pl.ds(pl.multiple_of(start + q * PART, PART), PART))
            return carry

        lax.fori_loop(0, size // PART, some, 0)

    def combine(c):
        def work(at):
            packed = jnp.zeros((PART, cols), half)
            below = later[rows - 1, at, :]
            for r in range(rows):
                here = later[r, at, :]
                s = state[r, at, :] + (here + below)
                state[r, at, :] = s
                packed = pack_row(packed, r, s, wlon[r, at, :])
                pack_edge(0, at, r, s)
                below = here
            edge_out[0, 1, at, :] = packed

        parts(c, work)
        send_edges(0, c)

    def advance(step, c):
        last = step == STEPS - 1
        src = state if step % 2 == 0 else later
        dst = out if last else later if step % 2 == 0 else state

        def work(at):
            both = jnp.where(
                lane % 2 == 0,
                edge_in[step, 0, at, :].astype(jnp.float32),
                pltpu.roll(edge_in[step, 1, at, :].astype(jnp.float32), 2, 1),
            ).astype(half)
            packed = jnp.zeros((PART, cols), half)
            centre = None
            below = edge_in[step, 3, at, :].astype(jnp.float32)
            for r in range(rows + 1):
                if r < rows:
                    s = src[r, at, :]
                    plus, minus = split(s, wlon[r, at, :])
                    moved = pltpu.roll(both, (cols - 1 - 2 * r) % cols, 1)
                    from_east = pltpu.roll(plus.astype(half), cols - 1, 1)
                    from_west = pltpu.roll(minus.astype(half), 1, 1)
                    across = (
                        (1.0 - 4.0 * RATE) * s
                        + jnp.where(at_east, moved, from_east).astype(jnp.float32)
                        + jnp.where(at_west, moved, from_west).astype(jnp.float32)
                    )
                    above, here = split(s, wlat[r, at, :])
                else:
                    above = edge_in[step, 2, at, :].astype(jnp.float32)
                if r > 0:
                    total = centre + above
                    dst[r - 1, at, :] = total
                    if not last:
                        packed = pack_row(packed, r - 1, total, wlon[r - 1, at, :])
                        pack_edge(step + 1, at, r - 1, total)
                if r < rows:
                    centre = across + below
                    below = here
            if not last:
                edge_out[step + 1, 1, at, :] = packed

        await_edges(step, c)
        parts(c, work)
        if not last:
            send_edges(step + 1, c)

    ship(1)
    lax.fori_loop(0, n_lon, read_meta, 0)
    deposit(0)
    for which, buf in enumerate((state, wlon, wlat)):
        pltpu.make_async_copy(buf, buf, load_sem.at[which]).wait()
    combine(0)
    ship(2)
    deposit(1)
    combine(1)
    ship(3)
    deposit(2)
    combine(2)
    advance(0, 0)
    deposit(3)
    combine(3)
    advance(0, 1)
    advance(1, 0)
    advance(0, 2)
    advance(1, 1)
    advance(0, 3)
    advance(1, 2)
    advance(1, 3)

    for c in range(len(chunks)):
        sent = send.at[pl.ds(0, n_dev - 1), pl.ds(*chunks[c])]
        pltpu.make_async_copy(sent, sent, send_sem.at[c]).wait()
    sent = meta_send.at[pl.ds(0, n_dev - 1)]
    pltpu.make_async_copy(sent, sent, meta_send_sem).wait()


def write_out(x, out, sem):
    def put(r, carry):
        pltpu.make_async_copy(x.at[r], out.at[:, r, :], sem).start()
        return carry

    lax.fori_loop(0, x.shape[0], put, 0)
    pltpu.make_async_copy(x, x, sem).wait()


def local(departures, footprint, channel_map, adjoint_in, wind_lon, wind_lat):
    n_lat, n_lon = lax.axis_size("lat"), lax.axis_size("lon")
    n_dev = n_lat * n_lon
    levels, rows, cols = adjoint_in.shape
    obs = departures.shape[0]
    capacity = 2 * obs // n_dev
    slots = -(-capacity // LANES) * LANES
    wide = min(n_dev * slots, max(4096, n_lat * slots))
    n_chunks = len(chunks_of(levels))
    block = pltpu.VMEM((n_dev, levels, slots), jnp.bfloat16)
    meta = pltpu.VMEM((n_dev, 1, slots), jnp.int32)
    field = pltpu.VMEM((rows, levels, cols), jnp.float32)
    edges = pltpu.VMEM((STEPS, 4, levels, cols), jnp.bfloat16)
    vmem, anywhere = pl.BlockSpec(memory_space=pltpu.VMEM), pl.BlockSpec(memory_space=pl.ANY)
    hbm = pl.BlockSpec(memory_space=pltpu.HBM)
    result = pl.pallas_call(
        functools.partial(kernel, n_lat, n_lon),
        out_shape=pltpu.VMEM((rows, levels, cols), jnp.float32),
        in_specs=[vmem, hbm, vmem] + [hbm] * 3,
        out_specs=vmem,
        scratch_shapes=[
            pltpu.VMEM(departures.shape, jnp.bfloat16),
            pltpu.VMEM((levels + META, obs), jnp.bfloat16),
            pltpu.VMEM((obs, slots), jnp.float32),
            block, block, meta, meta,
            pltpu.VMEM((n_dev * slots // wide, 2 * cols, wide), jnp.bfloat16),
            pltpu.VMEM((n_dev * slots // wide, rows // 2, 16, wide), jnp.bfloat16),
            field, field, field, field,
            edges, edges,
            pltpu.SemaphoreType.DMA((4,)),
            pltpu.SemaphoreType.DMA((n_chunks,)),
            pltpu.SemaphoreType.DMA((n_chunks, n_lon)),
            pltpu.SemaphoreType.DMA,
            pltpu.SemaphoreType.DMA((n_lon,)),
            pltpu.SemaphoreType.DMA((STEPS, n_chunks, 4)),
            pltpu.SemaphoreType.DMA((STEPS, n_chunks, 4)),
        ],
        compiler_params=pltpu.CompilerParams(
            collective_id=0, has_side_effects=True, vmem_limit_bytes=52 << 20
        ),
        name="assimilate",
    )(footprint.T, departures, channel_map, adjoint_in, wind_lon, wind_lat)
    return pl.pallas_call(
        write_out,
        out_shape=jax.ShapeDtypeStruct(adjoint_in.shape, jnp.float32),
        in_specs=[vmem],
        out_specs=hbm,
        scratch_shapes=[pltpu.SemaphoreType.DMA],
        compiler_params=pltpu.CompilerParams(vmem_limit_bytes=8 << 20),
        name="write_out",
    )(result)


def solution(mesh):
    in_specs = (
        P(("lat", "lon"), None),
        P(("lat", "lon"), None),
        P(),
        P(None, "lat", "lon"),
        P(None, "lat", "lon"),
        P(None, "lat", "lon"),
    )
    out_specs = P(None, "lat", "lon")
    return jax.shard_map(local, mesh=mesh, in_specs=in_specs, out_specs=out_specs, check_vma=False)
```

```python
import functools

import jax
import jax.numpy as jnp
from jax import lax
from jax.experimental import pallas as pl
from jax.experimental.pallas import tpu as pltpu
from jax.sharding import PartitionSpec as P

STEPS = 2
RATE = 0.2
LANES = 128
META = 16
PART = 16
MESH = pl.DeviceIdType.MESH


def log2(size):
    assert size & (size - 1) == 0
    return size.bit_length() - 1


def nt_dot(a, b):
    return lax.dot_general(a, b, (((1,), (1,)), ((), ())), preferred_element_type=jnp.float32)


def nn_dot(a, b):
    return lax.dot_general(a, b, (((1,), (0,)), ((), ())), preferred_element_type=jnp.float32)


def xor(n, v, mask):
    total = 0
    for bit in range(log2(n)):
        here, other = v // 2 ** bit % 2, mask // 2 ** bit % 2
        total = total + 2 ** bit * (here + other - 2 * here * other)
    return total


PARTS = (2, 2, 2, 2)


def chunks_of(levels):
    unit = levels // sum(PARTS)
    assert unit % PART == 0 and unit * sum(PARTS) == levels
    return [(unit * sum(PARTS[:c]), unit * size) for c, size in enumerate(PARTS)]


def kernel(
    n_lat, n_lon, foot, dep_hbm, cmap, adj_hbm, wlon_hbm, wlat_hbm, out,
    dep, prof, key, send, recv, meta_send, meta_recv, cell_hot, row_hot,
    state, later, wlon, wlat, edge_out, edge_in,
    load_sem, send_sem, recv_sem, meta_send_sem, meta_recv_sem, edge_send_sem, edge_recv_sem,
):
    lat, lon = lax.axis_index("lat"), lax.axis_index("lon")
    n_dev = n_lat * n_lon
    rows, levels, cols = state.shape
    obs = dep.shape[0]
    slots = recv.shape[2]
    depth = n_lat * slots
    chunks = chunks_of(levels)

    pltpu.make_async_copy(dep_hbm, dep, load_sem.at[3]).start()

    barrier = pltpu.get_barrier_semaphore()

    def greet(i, carry):
        pl.semaphore_signal(
            barrier, inc=1,
            device_id=((lat + i // n_lon) % n_lat, (lon + i % n_lon) % n_lon),
            device_id_type=MESH,
        )
        return carry

    lax.fori_loop(1, n_dev, greet, 0)

    def load(r, carry):
        pltpu.make_async_copy(adj_hbm.at[:, r, :], state.at[r], load_sem.at[0]).start()
        pltpu.make_async_copy(wlon_hbm.at[:, r, :], wlon.at[r], load_sem.at[1]).start()
        pltpu.make_async_copy(wlat_hbm.at[:, r, :], wlat.at[r], load_sem.at[2]).start()
        return carry

    shift_grid, shift_row, shift_col = log2(n_lon * cols), log2(rows), log2(cols)
    cells = foot[...]
    grid_row = lax.shift_right_logical(cells, shift_grid)
    grid_col = cells & (n_lon * cols - 1)
    owner = (
        lax.shift_right_logical(grid_row[0:1], shift_row) * n_lon
        + lax.shift_right_logical(grid_col[0:1], shift_col)
    )
    in_row = grid_row & (rows - 1)
    in_col = grid_col & (cols - 1)

    def base(cell):
        low = jnp.minimum(jnp.minimum(cell[0:1], cell[1:2]), jnp.minimum(cell[2:3], cell[3:4]))
        high = jnp.maximum(jnp.maximum(cell[0:1], cell[1:2]), jnp.maximum(cell[2:3], cell[3:4]))
        return jnp.where(high - low == 1, low, high)

    base_row, base_col = base(in_row), base(in_col)
    chunk = 256
    upper = jnp.where(
        lax.broadcasted_iota(jnp.int32, (chunk, chunk), 0)
        <= lax.broadcasted_iota(jnp.int32, (chunk, chunk), 1),
        1.0, 0.0,
    ).astype(jnp.bfloat16)
    owners = lax.broadcasted_iota(jnp.int32, (n_dev, chunk), 0)
    seen = jnp.zeros((n_dev, 1), jnp.float32)
    for start in range(0, obs, chunk):
        hot = jnp.where(owners == owner[:, start:start + chunk], 1.0, 0.0)
        count = jnp.dot(hot.astype(jnp.bfloat16), upper, preferred_element_type=jnp.float32) + seen
        place = jnp.sum(hot * count, axis=0, keepdims=True) - 1.0
        seen = count[:, chunk - 1:chunk]
        which = lax.broadcasted_iota(jnp.int32, (16, chunk), 0)
        pair = jnp.where(which == 0, owner[:, start:start + chunk].astype(jnp.float32), place)
        scale = jnp.where(lax.broadcasted_iota(jnp.int32, (16, slots), 0) == 0, slots, 1)
        scale = jnp.where(lax.broadcasted_iota(jnp.int32, (16, slots), 0) < 2, scale, 0)
        key[start:start + chunk, :] = lax.dot_general(
            pair.astype(jnp.bfloat16), scale.astype(jnp.float32).astype(jnp.bfloat16),
            (((0,), (0,)), ((), ())), preferred_element_type=jnp.float32,
        )

    pltpu.make_async_copy(dep_hbm, dep, load_sem.at[3]).wait()
    prof[0:levels, :] = lax.dot_general(
        cmap[...], dep[...], (((0,), (1,)), ((), ())), preferred_element_type=jnp.float32
    ).astype(jnp.bfloat16)
    which = lax.broadcasted_iota(jnp.int32, (META, obs), 0)
    prof[levels:levels + META, :] = jnp.where(
        which == 0, base_row, jnp.where(which == 1, base_col, 0)
    ).astype(jnp.float32).astype(jnp.bfloat16)

    @pl.when(lat == 0)
    def _():
        edge_in[:, 3] = jnp.zeros_like(edge_in[:, 3])

    @pl.when(lat == n_lat - 1)
    def _():
        edge_in[:, 2] = jnp.zeros_like(edge_in[:, 2])

    pl.semaphore_wait(barrier, n_dev - 1)

    own = n_lon - 1

    def target(k, a):
        return xor(n_lat, lat, a), xor(n_lon, lon, n_lon - 1 - k)

    def block_copy(c, k, a):
        i, (first, size) = k * n_lat + a, chunks[c]
        at = pl.ds(first, size)
        return pltpu.make_async_remote_copy(
            src_ref=send.at[i, at], dst_ref=recv.at[i, at],
            send_sem=send_sem.at[c], recv_sem=recv_sem.at[c, k],
            device_id=target(k, a), device_id_type=MESH,
        )

    def meta_copy(k, a):
        i = k * n_lat + a
        return pltpu.make_async_remote_copy(
            src_ref=meta_send.at[i], dst_ref=meta_recv.at[i],
            send_sem=meta_send_sem, recv_sem=meta_recv_sem.at[k],
            device_id=target(k, a), device_id_type=MESH,
        )

    def route(k, carry):
        lane = lax.broadcasted_iota(jnp.int32, (obs, slots), 1)
        hots = []
        for a in range(n_lat):
            to_lat, to_lon = target(k, a)
            wanted = (lane + (to_lat * n_lon + to_lon) * slots).astype(jnp.float32)
            hots.append(jnp.where(key[...] == wanted, 1.0, 0.0).astype(jnp.bfloat16))
        blocks = nn_dot(prof[...], jnp.concatenate(hots, axis=1))
        meta = (blocks[levels:levels + 1] * cols + blocks[levels + 1:levels + 2]).astype(jnp.int32)
        blocks = blocks[0:levels].astype(jnp.bfloat16)
        for a in range(n_lat):
            i = k * n_lat + a
            at = slice(a * slots, (a + 1) * slots)

            def away():
                send[i] = blocks[:, at]
                meta_send[i] = meta[:, at]
                block_copy(0, k, a).start()
                meta_copy(k, a).start()

            if a == 0:
                @pl.when(k == own)
                def _():
                    recv[i] = blocks[:, at]
                    meta_recv[i] = meta[:, at]

                pl.when(k != own)(away)
            else:
                away()
        lax.fori_loop(k * rows // n_lon, (k + 1) * rows // n_lon, load, 0)
        return carry

    lax.fori_loop(0, n_lon, route, 0)

    def ship(c):
        def some(k, carry):
            for a in range(n_lat):
                if a == 0:
                    @pl.when(k != own)
                    def _():
                        block_copy(c, k, 0).start()
                else:
                    block_copy(c, k, a).start()
            return carry

        lax.fori_loop(0, n_lon, some, 0)

    def await_group(k, ref, sem):
        @pl.when(k != own)
        def _():
            here = ref(pl.ds(k * n_lat, n_lat))
            pltpu.make_async_copy(here, here, sem).wait()

        @pl.when(k == own)
        def _():
            here = ref(pl.ds(k * n_lat + 1, n_lat - 1))
            pltpu.make_async_copy(here, here, sem).wait()

    wide = cell_hot.shape[2]
    groups = wide // depth

    def read_meta(k, carry):
        await_group(k, lambda i: meta_recv.at[i], meta_recv_sem.at[k])
        meta = jnp.concatenate([meta_recv[k * n_lat + a] for a in range(n_lat)], axis=1)
        at_row, at_col = lax.shift_right_logical(meta, shift_col), meta & (cols - 1)
        cell = lax.broadcasted_iota(jnp.int32, (2 * cols, depth), 0)
        first = at_row % 2 * cols
        block, at = k // groups, pl.ds(pl.multiple_of(k % groups * depth, depth), depth)
        cell_hot[block, :, at] = jnp.where(
            (cell == first + at_col) | (cell == first + ((at_col + 1) & (cols - 1))), 0.25, 0.0
        ).astype(jnp.bfloat16)
        pair = lax.shift_right_logical(at_row, 1)
        for p in range(rows // 2):
            hot = jnp.where(pair == p, 1.0, 0.0)
            row_hot[block, p, :, at] = jnp.broadcast_to(hot, (16, depth)).astype(jnp.bfloat16)
        return carry

    def deposit(c):
        start, size = chunks[c]
        at = pl.ds(start, size)
        tile = min(rows // 2, max(1, 512 // size))
        for block in range(n_lon // groups):
            def arrive(k, carry):
                await_group(k, lambda i: recv.at[i, at], recv_sem.at[c, k])
                return carry

            lax.fori_loop(block * groups, (block + 1) * groups, arrive, 0)
            first = block * groups * n_lat
            got = jnp.concatenate([recv[first + i, at, :] for i in range(groups * n_lat)], axis=1)
            stacked = got.reshape(size // 16, 16, wide)
            for t in range(rows // 2 // tile):
                lhs = []
                for j in range(tile):
                    lhs.append((stacked * row_hot[block, t * tile + j][None]).reshape(size, wide))
                found = nt_dot(jnp.concatenate(lhs, axis=0), cell_hot[block])
                for j in range(tile):
                    r = 2 * (t * tile + j)
                    here = found[j * size:(j + 1) * size]
                    low, high = here[:, 0:cols], here[:, cols:2 * cols]
                    if block > 0:
                        low, high = later[r, at, :] + low, later[r + 1, at, :] + high
                    later[r, at, :] = low
                    later[r + 1, at, :] = high

    assert 2 * rows <= cols and rows % 4 == 0
    half = jnp.bfloat16
    lane = lax.broadcasted_iota(jnp.int32, (PART, cols), 1)
    lane_half = lane.astype(jnp.float32).astype(half)
    side_half = jnp.where(lane == cols - 1, -0.5, 0.5)
    west, east = (lon + n_lon - 1) % n_lon, (lon + 1) % n_lon
    south, north = (lat + n_lat - 1) % n_lat, (lat + 1) % n_lat
    targets = ((lat, west), (lat, east), (south, lon), (north, lon))

    def edge_copy(step, c, side):
        at = pl.ds(*chunks[c])
        return pltpu.make_async_remote_copy(
            src_ref=edge_out.at[step, max(side, 1), at], dst_ref=edge_in.at[step, side, at],
            send_sem=edge_send_sem.at[step, c, side], recv_sem=edge_recv_sem.at[step, c, side],
            device_id=targets[side], device_id_type=MESH,
        )

    def send_edges(step, c):
        edge_copy(step, c, 0).start()
        edge_copy(step, c, 1).start()

        @pl.when(lat > 0)
        def _():
            edge_copy(step, c, 2).start()

        @pl.when(lat < n_lat - 1)
        def _():
            edge_copy(step, c, 3).start()

    def await_edges(step, c):
        edge_copy(step, c, 0).wait()
        edge_copy(step, c, 1).wait()

        @pl.when(lat > 0)
        def _():
            edge_copy(step, c, 2).wait_send()
            edge_copy(step, c, 3).wait_recv()

        @pl.when(lat < n_lat - 1)
        def _():
            edge_copy(step, c, 3).wait_send()
            edge_copy(step, c, 2).wait_recv()

    def split(s, w):
        flux = (0.5 * w) * s
        even = RATE * s
        return even + flux, even - flux

    def pack_row(packed, r, s, w):
        side = ((RATE + side_half * w) * s).astype(half)
        if r > 0:
            side = pltpu.roll(side, 2 * r, 1)
        here = (lane_half == half(2 * r)) | (lane_half == half((2 * r - 1) % cols))
        return jnp.where(here, side, packed)

    def pack_edge(step, at, r, s):
        if r == 0:
            edge_out[step, 2, at, :] = split(s, wlat[r, at, :])[0].astype(jnp.bfloat16)
        if r == rows - 1:
            edge_out[step, 3, at, :] = split(s, wlat[r, at, :])[1].astype(jnp.bfloat16)

    def parts(c, work):
        start, size = chunks[c]

        def some(q, carry):
            work(pl.ds(pl.multiple_of(start + q * PART, PART), PART))
            return carry

        lax.fori_loop(0, size // PART, some, 0)

    def combine(c):
        def work(at):
            packed = jnp.zeros((PART, cols), half)
            below = later[rows - 1, at, :]
            for r in range(rows):
                here = later[r, at, :]
                s = state[r, at, :] + (here + below)
                state[r, at, :] = s
                packed = pack_row(packed, r, s, wlon[r, at, :])
                pack_edge(0, at, r, s)
                below = here
            edge_out[0, 1, at, :] = packed

        parts(c, work)
        send_edges(0, c)

    def advance(step, c):
        last = step == STEPS - 1
        src = state if step % 2 == 0 else later
        dst = out if last else later if step % 2 == 0 else state

        def work(at):
            both = jnp.where(
                lane % 2 == 0,
                edge_in[step, 0, at, :].astype(jnp.float32),
                pltpu.roll(edge_in[step, 1, at, :].astype(jnp.float32), 2, 1),
            ).astype(half)
            packed = jnp.zeros((PART, cols), half)
            centre = None
            below = edge_in[step, 3, at, :].astype(jnp.float32)
            for r in range(rows + 1):
                if r < rows:
                    s = src[r, at, :]
                    plus, minus = split(s, wlon[r, at, :])
                    moved = pltpu.roll(both, (cols - 1 - 2 * r) % cols, 1)
                    moved = moved.astype(jnp.float32)
                    across = (
                        (1.0 - 4.0 * RATE) * s
                        + jnp.where(lane == cols - 1, moved, pltpu.roll(plus, cols - 1, 1))
                        + jnp.where(lane == 0, moved, pltpu.roll(minus, 1, 1))
                    )
                    above, here = split(s, wlat[r, at, :])
                else:
                    above = edge_in[step, 2, at, :].astype(jnp.float32)
                if r > 0:
                    total = centre + above
                    dst[r - 1, at, :] = total
                    if not last:
                        packed = pack_row(packed, r - 1, total, wlon[r - 1, at, :])
                        pack_edge(step + 1, at, r - 1, total)
                if r < rows:
                    centre = across + below
                    below = here
            if not last:
                edge_out[step + 1, 1, at, :] = packed

        await_edges(step, c)
        parts(c, work)
        if not last:
            send_edges(step + 1, c)

    n_chunks = len(chunks)
    for c in range(1, n_chunks):
        ship(c)
    lax.fori_loop(0, n_lon, read_meta, 0)
    for which, buf in enumerate((state, wlon, wlat)):
        pltpu.make_async_copy(buf, buf, load_sem.at[which]).wait()
    for c in range(n_chunks):
        deposit(c)
        combine(c)
    for step in range(STEPS):
        for c in range(n_chunks):
            advance(step, c)

    for c in range(len(chunks)):
        sent = send.at[pl.ds(0, n_dev - 1), pl.ds(*chunks[c])]
        pltpu.make_async_copy(sent, sent, send_sem.at[c]).wait()
    sent = meta_send.at[pl.ds(0, n_dev - 1)]
    pltpu.make_async_copy(sent, sent, meta_send_sem).wait()


def write_out(x, out, sem):
    def put(r, carry):
        pltpu.make_async_copy(x.at[r], out.at[:, r, :], sem).start()
        return carry

    lax.fori_loop(0, x.shape[0], put, 0)
    pltpu.make_async_copy(x, x, sem).wait()


def local(departures, footprint, channel_map, adjoint_in, wind_lon, wind_lat):
    n_lat, n_lon = lax.axis_size("lat"), lax.axis_size("lon")
    n_dev = n_lat * n_lon
    levels, rows, cols = adjoint_in.shape
    obs = departures.shape[0]
    capacity = 2 * obs // n_dev
    slots = -(-capacity // LANES) * LANES
    wide = min(n_dev * slots, max(4096, n_lat * slots))
    n_chunks = len(chunks_of(levels))
    block = pltpu.VMEM((n_dev, levels, slots), jnp.bfloat16)
    meta = pltpu.VMEM((n_dev, 1, slots), jnp.int32)
    field = pltpu.VMEM((rows, levels, cols), jnp.float32)
    edges = pltpu.VMEM((STEPS, 4, levels, cols), jnp.bfloat16)
    vmem, anywhere = pl.BlockSpec(memory_space=pltpu.VMEM), pl.BlockSpec(memory_space=pl.ANY)
    hbm = pl.BlockSpec(memory_space=pltpu.HBM)
    result = pl.pallas_call(
        functools.partial(kernel, n_lat, n_lon),
        out_shape=pltpu.VMEM((rows, levels, cols), jnp.float32),
        in_specs=[vmem, hbm, vmem] + [hbm] * 3,
        out_specs=vmem,
        scratch_shapes=[
            pltpu.VMEM(departures.shape, jnp.bfloat16),
            pltpu.VMEM((levels + META, obs), jnp.bfloat16),
            pltpu.VMEM((obs, slots), jnp.float32),
            block, block, meta, meta,
            pltpu.VMEM((n_dev * slots // wide, 2 * cols, wide), jnp.bfloat16),
            pltpu.VMEM((n_dev * slots // wide, rows // 2, 16, wide), jnp.bfloat16),
            field, field, field, field,
            edges, edges,
            pltpu.SemaphoreType.DMA((4,)),
            pltpu.SemaphoreType.DMA((n_chunks,)),
            pltpu.SemaphoreType.DMA((n_chunks, n_lon)),
            pltpu.SemaphoreType.DMA,
            pltpu.SemaphoreType.DMA((n_lon,)),
            pltpu.SemaphoreType.DMA((STEPS, n_chunks, 4)),
            pltpu.SemaphoreType.DMA((STEPS, n_chunks, 4)),
        ],
        compiler_params=pltpu.CompilerParams(
            collective_id=0, has_side_effects=True, vmem_limit_bytes=52 << 20
        ),
        name="assimilate",
    )(footprint.T, departures, channel_map, adjoint_in, wind_lon, wind_lat)
    return pl.pallas_call(
        write_out,
        out_shape=jax.ShapeDtypeStruct(adjoint_in.shape, jnp.float32),
        in_specs=[vmem],
        out_specs=hbm,
        scratch_shapes=[pltpu.SemaphoreType.DMA],
        compiler_params=pltpu.CompilerParams(vmem_limit_bytes=8 << 20),
        name="write_out",
    )(result)


def solution(mesh):
    in_specs = (
        P(("lat", "lon"), None),
        P(("lat", "lon"), None),
        P(),
        P(None, "lat", "lon"),
        P(None, "lat", "lon"),
        P(None, "lat", "lon"),
    )
    out_specs = P(None, "lat", "lon")
    return jax.shard_map(local, mesh=mesh, in_specs=in_specs, out_specs=out_specs, check_vma=False)
```

```python
import functools

import jax
import jax.numpy as jnp
from jax import lax
from jax.experimental import pallas as pl
from jax.experimental.pallas import tpu as pltpu
from jax.sharding import PartitionSpec as P

STEPS = 2
RATE = 0.2
LANES = 128
META = 16
PART = 16
MESH = pl.DeviceIdType.MESH


def log2(size):
    assert size & (size - 1) == 0
    return size.bit_length() - 1


def nt_dot(a, b):
    return lax.dot_general(a, b, (((1,), (1,)), ((), ())), preferred_element_type=jnp.float32)


def nn_dot(a, b):
    return lax.dot_general(a, b, (((1,), (0,)), ((), ())), preferred_element_type=jnp.float32)


def xor(n, v, mask):
    total = 0
    for bit in range(log2(n)):
        here, other = v // 2 ** bit % 2, mask // 2 ** bit % 2
        total = total + 2 ** bit * (here + other - 2 * here * other)
    return total


PARTS = (2, 2, 2, 2)


def chunks_of(levels):
    unit = levels // sum(PARTS)
    assert unit % PART == 0 and unit * sum(PARTS) == levels
    return [(unit * sum(PARTS[:c]), unit * size) for c, size in enumerate(PARTS)]


def kernel(
    n_lat, n_lon, foot, dep_hbm, cmap, adj_hbm, wlon_hbm, wlat_hbm, out,
    dep, prof, key, send, recv, meta_send, meta_recv, cell_hot, row_hot,
    state, later, wlon, wlat, edge_out, edge_in,
    load_sem, send_sem, recv_sem, meta_send_sem, meta_recv_sem, edge_send_sem, edge_recv_sem,
):
    lat, lon = lax.axis_index("lat"), lax.axis_index("lon")
    n_dev = n_lat * n_lon
    rows, levels, cols = state.shape
    obs = dep.shape[0]
    slots = recv.shape[2]
    depth = n_lat * slots
    chunks = chunks_of(levels)

    pltpu.make_async_copy(dep_hbm, dep, load_sem.at[3]).start()

    barrier = pltpu.get_barrier_semaphore()

    def greet(i, carry):
        pl.semaphore_signal(
            barrier, inc=1,
            device_id=((lat + i // n_lon) % n_lat, (lon + i % n_lon) % n_lon),
            device_id_type=MESH,
        )
        return carry

    lax.fori_loop(1, n_dev, greet, 0)

    def load(r, carry):
        pltpu.make_async_copy(adj_hbm.at[:, r, :], state.at[r], load_sem.at[0]).start()
        pltpu.make_async_copy(wlon_hbm.at[:, r, :], wlon.at[r], load_sem.at[1]).start()
        pltpu.make_async_copy(wlat_hbm.at[:, r, :], wlat.at[r], load_sem.at[2]).start()
        return carry

    shift_grid, shift_row, shift_col = log2(n_lon * cols), log2(rows), log2(cols)
    cells = foot[...]
    grid_row = lax.shift_right_logical(cells, shift_grid)
    grid_col = cells & (n_lon * cols - 1)
    owner = (
        lax.shift_right_logical(grid_row[0:1], shift_row) * n_lon
        + lax.shift_right_logical(grid_col[0:1], shift_col)
    )
    in_row = grid_row & (rows - 1)
    in_col = grid_col & (cols - 1)

    def base(cell):
        low = jnp.minimum(jnp.minimum(cell[0:1], cell[1:2]), jnp.minimum(cell[2:3], cell[3:4]))
        high = jnp.maximum(jnp.maximum(cell[0:1], cell[1:2]), jnp.maximum(cell[2:3], cell[3:4]))
        return jnp.where(high - low == 1, low, high)

    base_row, base_col = base(in_row), base(in_col)
    chunk = 256
    upper = jnp.where(
        lax.broadcasted_iota(jnp.int32, (chunk, chunk), 0)
        <= lax.broadcasted_iota(jnp.int32, (chunk, chunk), 1),
        1.0, 0.0,
    ).astype(jnp.bfloat16)
    owners = lax.broadcasted_iota(jnp.int32, (n_dev, chunk), 0)
    seen = jnp.zeros((n_dev, 1), jnp.float32)
    for start in range(0, obs, chunk):
        hot = jnp.where(owners == owner[:, start:start + chunk], 1.0, 0.0)
        count = jnp.dot(hot.astype(jnp.bfloat16), upper, preferred_element_type=jnp.float32) + seen
        place = jnp.sum(hot * count, axis=0, keepdims=True) - 1.0
        seen = count[:, chunk - 1:chunk]
        which = lax.broadcasted_iota(jnp.int32, (16, chunk), 0)
        pair = jnp.where(which == 0, owner[:, start:start + chunk].astype(jnp.float32), place)
        scale = jnp.where(lax.broadcasted_iota(jnp.int32, (16, slots), 0) == 0, slots, 1)
        scale = jnp.where(lax.broadcasted_iota(jnp.int32, (16, slots), 0) < 2, scale, 0)
        key[start:start + chunk, :] = lax.dot_general(
            pair.astype(jnp.bfloat16), scale.astype(jnp.float32).astype(jnp.bfloat16),
            (((0,), (0,)), ((), ())), preferred_element_type=jnp.float32,
        )

    pltpu.make_async_copy(dep_hbm, dep, load_sem.at[3]).wait()
    prof[0:levels, :] = lax.dot_general(
        cmap[...], dep[...], (((0,), (1,)), ((), ())), preferred_element_type=jnp.float32
    ).astype(jnp.bfloat16)
    which = lax.broadcasted_iota(jnp.int32, (META, obs), 0)
    prof[levels:levels + META, :] = jnp.where(
        which == 0, base_row, jnp.where(which == 1, base_col, 0)
    ).astype(jnp.float32).astype(jnp.bfloat16)

    @pl.when(lat == 0)
    def _():
        edge_in[:, 3] = jnp.zeros_like(edge_in[:, 3])

    @pl.when(lat == n_lat - 1)
    def _():
        edge_in[:, 2] = jnp.zeros_like(edge_in[:, 2])

    pl.semaphore_wait(barrier, n_dev - 1)

    own = n_lon // 2

    def target(k, a):
        return xor(n_lat, lat, a), xor(n_lon, lon, (k + n_lon // 2) % n_lon)

    def block_copy(c, k, a):
        i, (first, size) = k * n_lat + a, chunks[c]
        at = pl.ds(first, size)
        return pltpu.make_async_remote_copy(
            src_ref=send.at[i, at], dst_ref=recv.at[i, at],
            send_sem=send_sem.at[c], recv_sem=recv_sem.at[c, k],
            device_id=target(k, a), device_id_type=MESH,
        )

    def meta_copy(k, a):
        i = k * n_lat + a
        return pltpu.make_async_remote_copy(
            src_ref=meta_send.at[i], dst_ref=meta_recv.at[i],
            send_sem=meta_send_sem, recv_sem=meta_recv_sem.at[k],
            device_id=target(k, a), device_id_type=MESH,
        )

    def route(k, carry):
        lane = lax.broadcasted_iota(jnp.int32, (obs, slots), 1)
        hots = []
        for a in range(n_lat):
            to_lat, to_lon = target(k, a)
            wanted = (lane + (to_lat * n_lon + to_lon) * slots).astype(jnp.float32)
            hots.append(jnp.where(key[...] == wanted, 1.0, 0.0).astype(jnp.bfloat16))
        blocks = nn_dot(prof[...], jnp.concatenate(hots, axis=1))
        meta = (blocks[levels:levels + 1] * cols + blocks[levels + 1:levels + 2]).astype(jnp.int32)
        blocks = blocks[0:levels].astype(jnp.bfloat16)
        for a in range(n_lat):
            i = k * n_lat + a
            at = slice(a * slots, (a + 1) * slots)

            def away():
                send[i] = blocks[:, at]
                meta_send[i] = meta[:, at]
                block_copy(0, k, a).start()
                meta_copy(k, a).start()

            if a == 0:
                @pl.when(k == own)
                def _():
                    recv[i] = blocks[:, at]
                    meta_recv[i] = meta[:, at]

                pl.when(k != own)(away)
            else:
                away()
        lax.fori_loop(k * rows // n_lon, (k + 1) * rows // n_lon, load, 0)
        return carry

    lax.fori_loop(0, n_lon, route, 0)

    def ship(c):
        def some(k, carry):
            for a in range(n_lat):
                if a == 0:
                    @pl.when(k != own)
                    def _():
                        block_copy(c, k, 0).start()
                else:
                    block_copy(c, k, a).start()
            return carry

        lax.fori_loop(0, n_lon, some, 0)

    def await_group(k, ref, sem):
        @pl.when(k != own)
        def _():
            here = ref(pl.ds(k * n_lat, n_lat))
            pltpu.make_async_copy(here, here, sem).wait()

        @pl.when(k == own)
        def _():
            here = ref(pl.ds(k * n_lat + 1, n_lat - 1))
            pltpu.make_async_copy(here, here, sem).wait()

    wide = cell_hot.shape[2]
    groups = wide // depth

    def read_meta(k, carry):
        await_group(k, lambda i: meta_recv.at[i], meta_recv_sem.at[k])
        meta = jnp.concatenate([meta_recv[k * n_lat + a] for a in range(n_lat)], axis=1)
        at_row, at_col = lax.shift_right_logical(meta, shift_col), meta & (cols - 1)
        cell = lax.broadcasted_iota(jnp.int32, (2 * cols, depth), 0)
        first = at_row % 2 * cols
        block, at = k // groups, pl.ds(pl.multiple_of(k % groups * depth, depth), depth)
        cell_hot[block, :, at] = jnp.where(
            (cell == first + at_col) | (cell == first + ((at_col + 1) & (cols - 1))), 0.25, 0.0
        ).astype(jnp.bfloat16)
        pair = lax.shift_right_logical(at_row, 1)
        for p in range(rows // 2):
            hot = jnp.where(pair == p, 1.0, 0.0)
            row_hot[block, p, :, at] = jnp.broadcast_to(hot, (16, depth)).astype(jnp.bfloat16)
        return carry

    def deposit(c):
        start, size = chunks[c]
        at = pl.ds(start, size)
        tile = min(rows // 2, max(1, 512 // size))
        for block in range(n_lon // groups):
            def arrive(k, carry):
                await_group(k, lambda i: recv.at[i, at], recv_sem.at[c, k])
                return carry

            lax.fori_loop(block * groups, (block + 1) * groups, arrive, 0)
            first = block * groups * n_lat
            got = jnp.concatenate([recv[first + i, at, :] for i in range(groups * n_lat)], axis=1)
            stacked = got.reshape(size // 16, 16, wide)
            for t in range(rows // 2 // tile):
                lhs = []
                for j in range(tile):
                    lhs.append((stacked * row_hot[block, t * tile + j][None]).reshape(size, wide))
                found = nt_dot(jnp.concatenate(lhs, axis=0), cell_hot[block])
                for j in range(tile):
                    r = 2 * (t * tile + j)
                    here = found[j * size:(j + 1) * size]
                    low, high = here[:, 0:cols], here[:, cols:2 * cols]
                    if block > 0:
                        low, high = later[r, at, :] + low, later[r + 1, at, :] + high
                    later[r, at, :] = low
                    later[r + 1, at, :] = high

    assert 2 * rows <= cols and rows % 4 == 0
    half = jnp.bfloat16
    lane = lax.broadcasted_iota(jnp.int32, (PART, cols), 1)
    lane_half = lane.astype(jnp.float32).astype(half)
    side_half = jnp.where(lane == cols - 1, -0.5, 0.5)
    west, east = (lon + n_lon - 1) % n_lon, (lon + 1) % n_lon
    south, north = (lat + n_lat - 1) % n_lat, (lat + 1) % n_lat
    targets = ((lat, west), (lat, east), (south, lon), (north, lon))

    def edge_copy(step, c, side):
        at = pl.ds(*chunks[c])
        return pltpu.make_async_remote_copy(
            src_ref=edge_out.at[step, max(side, 1), at], dst_ref=edge_in.at[step, side, at],
            send_sem=edge_send_sem.at[step, c, side], recv_sem=edge_recv_sem.at[step, c, side],
            device_id=targets[side], device_id_type=MESH,
        )

    def send_edges(step, c):
        edge_copy(step, c, 0).start()
        edge_copy(step, c, 1).start()

        @pl.when(lat > 0)
        def _():
            edge_copy(step, c, 2).start()

        @pl.when(lat < n_lat - 1)
        def _():
            edge_copy(step, c, 3).start()

    def await_edges(step, c):
        edge_copy(step, c, 0).wait()
        edge_copy(step, c, 1).wait()

        @pl.when(lat > 0)
        def _():
            edge_copy(step, c, 2).wait_send()
            edge_copy(step, c, 3).wait_recv()

        @pl.when(lat < n_lat - 1)
        def _():
            edge_copy(step, c, 3).wait_send()
            edge_copy(step, c, 2).wait_recv()

    def split(s, w):
        flux = (0.5 * w) * s
        even = RATE * s
        return even + flux, even - flux

    def pack_row(packed, r, s, w):
        side = ((RATE + side_half * w) * s).astype(half)
        if r > 0:
            side = pltpu.roll(side, 2 * r, 1)
        here = (lane_half == half(2 * r)) | (lane_half == half((2 * r - 1) % cols))
        return jnp.where(here, side, packed)

    def pack_edge(step, at, r, s):
        if r == 0:
            edge_out[step, 2, at, :] = split(s, wlat[r, at, :])[0].astype(jnp.bfloat16)
        if r == rows - 1:
            edge_out[step, 3, at, :] = split(s, wlat[r, at, :])[1].astype(jnp.bfloat16)

    def parts(c, work):
        start, size = chunks[c]

        def some(q, carry):
            work(pl.ds(pl.multiple_of(start + q * PART, PART), PART))
            return carry

        lax.fori_loop(0, size // PART, some, 0)

    def combine(c):
        def work(at):
            packed = jnp.zeros((PART, cols), half)
            below = later[rows - 1, at, :]
            for r in range(rows):
                here = later[r, at, :]
                s = state[r, at, :] + (here + below)
                state[r, at, :] = s
                packed = pack_row(packed, r, s, wlon[r, at, :])
                pack_edge(0, at, r, s)
                below = here
            edge_out[0, 1, at, :] = packed

        parts(c, work)
        send_edges(0, c)

    def advance(step, c):
        last = step == STEPS - 1
        src = state if step % 2 == 0 else later
        dst = out if last else later if step % 2 == 0 else state

        def work(at):
            both = jnp.where(
                lane % 2 == 0,
                edge_in[step, 0, at, :].astype(jnp.float32),
                pltpu.roll(edge_in[step, 1, at, :].astype(jnp.float32), 2, 1),
            ).astype(half)
            packed = jnp.zeros((PART, cols), half)
            centre = None
            below = edge_in[step, 3, at, :].astype(jnp.float32)
            for r in range(rows + 1):
                if r < rows:
                    s = src[r, at, :]
                    plus, minus = split(s, wlon[r, at, :])
                    moved = pltpu.roll(both, (cols - 1 - 2 * r) % cols, 1)
                    moved = moved.astype(jnp.float32)
                    across = (
                        (1.0 - 4.0 * RATE) * s
                        + jnp.where(lane == cols - 1, moved, pltpu.roll(plus, cols - 1, 1))
                        + jnp.where(lane == 0, moved, pltpu.roll(minus, 1, 1))
                    )
                    above, here = split(s, wlat[r, at, :])
                else:
                    above = edge_in[step, 2, at, :].astype(jnp.float32)
                if r > 0:
                    total = centre + above
                    dst[r - 1, at, :] = total
                    if not last:
                        packed = pack_row(packed, r - 1, total, wlon[r - 1, at, :])
                        pack_edge(step + 1, at, r - 1, total)
                if r < rows:
                    centre = across + below
                    below = here
            if not last:
                edge_out[step + 1, 1, at, :] = packed

        await_edges(step, c)
        parts(c, work)
        if not last:
            send_edges(step + 1, c)

    n_chunks = len(chunks)
    for c in range(1, n_chunks):
        ship(c)
    lax.fori_loop(0, n_lon, read_meta, 0)
    for which, buf in enumerate((state, wlon, wlat)):
        pltpu.make_async_copy(buf, buf, load_sem.at[which]).wait()
    for c in range(n_chunks):
        deposit(c)
        combine(c)
    for step in range(STEPS):
        for c in range(n_chunks):
            advance(step, c)

    for c in range(len(chunks)):
        sent = send.at[pl.ds(0, n_dev - 1), pl.ds(*chunks[c])]
        pltpu.make_async_copy(sent, sent, send_sem.at[c]).wait()
    sent = meta_send.at[pl.ds(0, n_dev - 1)]
    pltpu.make_async_copy(sent, sent, meta_send_sem).wait()


def write_out(x, out, sem):
    def put(r, carry):
        pltpu.make_async_copy(x.at[r], out.at[:, r, :], sem).start()
        return carry

    lax.fori_loop(0, x.shape[0], put, 0)
    pltpu.make_async_copy(x, x, sem).wait()


def local(departures, footprint, channel_map, adjoint_in, wind_lon, wind_lat):
    n_lat, n_lon = lax.axis_size("lat"), lax.axis_size("lon")
    n_dev = n_lat * n_lon
    levels, rows, cols = adjoint_in.shape
    obs = departures.shape[0]
    capacity = 2 * obs // n_dev
    slots = -(-capacity // LANES) * LANES
    wide = min(n_dev * slots, max(4096, n_lat * slots))
    n_chunks = len(chunks_of(levels))
    block = pltpu.VMEM((n_dev, levels, slots), jnp.bfloat16)
    meta = pltpu.VMEM((n_dev, 1, slots), jnp.int32)
    field = pltpu.VMEM((rows, levels, cols), jnp.float32)
    edges = pltpu.VMEM((STEPS, 4, levels, cols), jnp.bfloat16)
    vmem, anywhere = pl.BlockSpec(memory_space=pltpu.VMEM), pl.BlockSpec(memory_space=pl.ANY)
    hbm = pl.BlockSpec(memory_space=pltpu.HBM)
    result = pl.pallas_call(
        functools.partial(kernel, n_lat, n_lon),
        out_shape=pltpu.VMEM((rows, levels, cols), jnp.float32),
        in_specs=[vmem, hbm, vmem] + [hbm] * 3,
        out_specs=vmem,
        scratch_shapes=[
            pltpu.VMEM(departures.shape, jnp.bfloat16),
            pltpu.VMEM((levels + META, obs), jnp.bfloat16),
            pltpu.VMEM((obs, slots), jnp.float32),
            block, block, meta, meta,
            pltpu.VMEM((n_dev * slots // wide, 2 * cols, wide), jnp.bfloat16),
            pltpu.VMEM((n_dev * slots // wide, rows // 2, 16, wide), jnp.bfloat16),
            field, field, field, field,
            edges, edges,
            pltpu.SemaphoreType.DMA((4,)),
            pltpu.SemaphoreType.DMA((n_chunks,)),
            pltpu.SemaphoreType.DMA((n_chunks, n_lon)),
            pltpu.SemaphoreType.DMA,
            pltpu.SemaphoreType.DMA((n_lon,)),
            pltpu.SemaphoreType.DMA((STEPS, n_chunks, 4)),
            pltpu.SemaphoreType.DMA((STEPS, n_chunks, 4)),
        ],
        compiler_params=pltpu.CompilerParams(
            collective_id=0, has_side_effects=True, vmem_limit_bytes=52 << 20
        ),
        name="assimilate",
    )(footprint.T, departures, channel_map, adjoint_in, wind_lon, wind_lat)
    return pl.pallas_call(
        write_out,
        out_shape=jax.ShapeDtypeStruct(adjoint_in.shape, jnp.float32),
        in_specs=[vmem],
        out_specs=hbm,
        scratch_shapes=[pltpu.SemaphoreType.DMA],
        compiler_params=pltpu.CompilerParams(vmem_limit_bytes=8 << 20),
        name="write_out",
    )(result)


def solution(mesh):
    in_specs = (
        P(("lat", "lon"), None),
        P(("lat", "lon"), None),
        P(),
        P(None, "lat", "lon"),
        P(None, "lat", "lon"),
        P(None, "lat", "lon"),
    )
    out_specs = P(None, "lat", "lon")
    return jax.shard_map(local, mesh=mesh, in_specs=in_specs, out_specs=out_specs, check_vma=False)
```

```python
import functools

import jax
import jax.numpy as jnp
from jax import lax
from jax.experimental import pallas as pl
from jax.experimental.pallas import tpu as pltpu
from jax.sharding import PartitionSpec as P

STEPS = 2
RATE = 0.2
LANES = 128
META = 16
PART = 16
MESH = pl.DeviceIdType.MESH


def log2(size):
    assert size & (size - 1) == 0
    return size.bit_length() - 1


def nt_dot(a, b):
    return lax.dot_general(a, b, (((1,), (1,)), ((), ())), preferred_element_type=jnp.float32)


def nn_dot(a, b):
    return lax.dot_general(a, b, (((1,), (0,)), ((), ())), preferred_element_type=jnp.float32)


def xor(n, v, mask):
    total = 0
    for bit in range(log2(n)):
        here, other = v // 2 ** bit % 2, mask // 2 ** bit % 2
        total = total + 2 ** bit * (here + other - 2 * here * other)
    return total


PARTS = (3, 2, 2, 1)


def chunks_of(levels):
    unit = levels // sum(PARTS)
    assert unit % PART == 0 and unit * sum(PARTS) == levels
    return [(unit * sum(PARTS[:c]), unit * size) for c, size in enumerate(PARTS)]


def kernel(
    n_lat, n_lon, foot, dep_hbm, cmap, adj_hbm, wlon_hbm, wlat_hbm, out,
    dep, prof, key, send, recv, meta_send, meta_recv, cell_hot, row_hot,
    state, later, wlon, wlat, edge_out, edge_in,
    load_sem, send_sem, recv_sem, meta_send_sem, meta_recv_sem, edge_send_sem, edge_recv_sem,
):
    lat, lon = lax.axis_index("lat"), lax.axis_index("lon")
    n_dev = n_lat * n_lon
    rows, levels, cols = state.shape
    obs = dep.shape[0]
    slots = recv.shape[2]
    depth = n_lat * slots
    chunks = chunks_of(levels)

    pltpu.make_async_copy(dep_hbm, dep, load_sem.at[3]).start()

    barrier = pltpu.get_barrier_semaphore()

    def greet(i, carry):
        pl.semaphore_signal(
            barrier, inc=1,
            device_id=((lat + i // n_lon) % n_lat, (lon + i % n_lon) % n_lon),
            device_id_type=MESH,
        )
        return carry

    lax.fori_loop(1, n_dev, greet, 0)

    def load(r, carry):
        pltpu.make_async_copy(adj_hbm.at[:, r, :], state.at[r], load_sem.at[0]).start()
        pltpu.make_async_copy(wlon_hbm.at[:, r, :], wlon.at[r], load_sem.at[1]).start()
        pltpu.make_async_copy(wlat_hbm.at[:, r, :], wlat.at[r], load_sem.at[2]).start()
        return carry

    shift_grid, shift_row, shift_col = log2(n_lon * cols), log2(rows), log2(cols)
    cells = foot[...]
    grid_row = lax.shift_right_logical(cells, shift_grid)
    grid_col = cells & (n_lon * cols - 1)
    owner = (
        lax.shift_right_logical(grid_row[0:1], shift_row) * n_lon
        + lax.shift_right_logical(grid_col[0:1], shift_col)
    )
    in_row = grid_row & (rows - 1)
    in_col = grid_col & (cols - 1)

    def base(cell):
        low = jnp.minimum(jnp.minimum(cell[0:1], cell[1:2]), jnp.minimum(cell[2:3], cell[3:4]))
        high = jnp.maximum(jnp.maximum(cell[0:1], cell[1:2]), jnp.maximum(cell[2:3], cell[3:4]))
        return jnp.where(high - low == 1, low, high)

    base_row, base_col = base(in_row), base(in_col)
    chunk = 256
    upper = jnp.where(
        lax.broadcasted_iota(jnp.int32, (chunk, chunk), 0)
        <= lax.broadcasted_iota(jnp.int32, (chunk, chunk), 1),
        1.0, 0.0,
    ).astype(jnp.bfloat16)
    owners = lax.broadcasted_iota(jnp.int32, (n_dev, chunk), 0)
    seen = jnp.zeros((n_dev, 1), jnp.float32)
    for start in range(0, obs, chunk):
        hot = jnp.where(owners == owner[:, start:start + chunk], 1.0, 0.0)
        count = jnp.dot(hot.astype(jnp.bfloat16), upper, preferred_element_type=jnp.float32) + seen
        place = jnp.sum(hot * count, axis=0, keepdims=True) - 1.0
        seen = count[:, chunk - 1:chunk]
        which = lax.broadcasted_iota(jnp.int32, (16, chunk), 0)
        pair = jnp.where(which == 0, owner[:, start:start + chunk].astype(jnp.float32), place)
        scale = jnp.where(lax.broadcasted_iota(jnp.int32, (16, slots), 0) == 0, slots, 1)
        scale = jnp.where(lax.broadcasted_iota(jnp.int32, (16, slots), 0) < 2, scale, 0)
        key[start:start + chunk, :] = lax.dot_general(
            pair.astype(jnp.bfloat16), scale.astype(jnp.float32).astype(jnp.bfloat16),
            (((0,), (0,)), ((), ())), preferred_element_type=jnp.float32,
        )

    pltpu.make_async_copy(dep_hbm, dep, load_sem.at[3]).wait()
    prof[0:levels, :] = lax.dot_general(
        cmap[...], dep[...], (((0,), (1,)), ((), ())), preferred_element_type=jnp.float32
    ).astype(jnp.bfloat16)
    which = lax.broadcasted_iota(jnp.int32, (META, obs), 0)
    prof[levels:levels + META, :] = jnp.where(
        which == 0, base_row, jnp.where(which == 1, base_col, 0)
    ).astype(jnp.float32).astype(jnp.bfloat16)

    @pl.when(lat == 0)
    def _():
        edge_in[:, 3] = jnp.zeros_like(edge_in[:, 3])

    @pl.when(lat == n_lat - 1)
    def _():
        edge_in[:, 2] = jnp.zeros_like(edge_in[:, 2])

    pl.semaphore_wait(barrier, n_dev - 1)

    own = n_lon // 2

    def target(k, a):
        return xor(n_lat, lat, a), xor(n_lon, lon, (k + n_lon // 2) % n_lon)

    def block_copy(c, k, a):
        i, (first, size) = k * n_lat + a, chunks[c]
        at = pl.ds(first, size)
        return pltpu.make_async_remote_copy(
            src_ref=send.at[i, at], dst_ref=recv.at[i, at],
            send_sem=send_sem.at[c], recv_sem=recv_sem.at[c, k],
            device_id=target(k, a), device_id_type=MESH,
        )

    def meta_copy(k, a):
        i = k * n_lat + a
        return pltpu.make_async_remote_copy(
            src_ref=meta_send.at[i], dst_ref=meta_recv.at[i],
            send_sem=meta_send_sem, recv_sem=meta_recv_sem.at[k],
            device_id=target(k, a), device_id_type=MESH,
        )

    def route(k, carry):
        lane = lax.broadcasted_iota(jnp.int32, (obs, slots), 1)
        hots = []
        for a in range(n_lat):
            to_lat, to_lon = target(k, a)
            wanted = (lane + (to_lat * n_lon + to_lon) * slots).astype(jnp.float32)
            hots.append(jnp.where(key[...] == wanted, 1.0, 0.0).astype(jnp.bfloat16))
        blocks = nn_dot(prof[...], jnp.concatenate(hots, axis=1))
        meta = (blocks[levels:levels + 1] * cols + blocks[levels + 1:levels + 2]).astype(jnp.int32)
        blocks = blocks[0:levels].astype(jnp.bfloat16)
        for a in range(n_lat):
            i = k * n_lat + a
            at = slice(a * slots, (a + 1) * slots)

            def away():
                send[i] = blocks[:, at]
                meta_send[i] = meta[:, at]
                block_copy(0, k, a).start()
                meta_copy(k, a).start()

            if a == 0:
                @pl.when(k == own)
                def _():
                    recv[i] = blocks[:, at]
                    meta_recv[i] = meta[:, at]

                pl.when(k != own)(away)
            else:
                away()
        lax.fori_loop(k * rows // n_lon, (k + 1) * rows // n_lon, load, 0)
        return carry

    lax.fori_loop(0, n_lon, route, 0)

    def ship(c):
        def some(k, carry):
            for a in range(n_lat):
                if a == 0:
                    @pl.when(k != own)
                    def _():
                        block_copy(c, k, 0).start()
                else:
                    block_copy(c, k, a).start()
            return carry

        lax.fori_loop(0, n_lon, some, 0)

    def await_group(k, ref, sem):
        @pl.when(k != own)
        def _():
            here = ref(pl.ds(k * n_lat, n_lat))
            pltpu.make_async_copy(here, here, sem).wait()

        @pl.when(k == own)
        def _():
            here = ref(pl.ds(k * n_lat + 1, n_lat - 1))
            pltpu.make_async_copy(here, here, sem).wait()

    wide = cell_hot.shape[2]
    groups = wide // depth

    def read_meta(k, carry):
        await_group(k, lambda i: meta_recv.at[i], meta_recv_sem.at[k])
        meta = jnp.concatenate([meta_recv[k * n_lat + a] for a in range(n_lat)], axis=1)
        at_row, at_col = lax.shift_right_logical(meta, shift_col), meta & (cols - 1)
        cell = lax.broadcasted_iota(jnp.int32, (2 * cols, depth), 0)
        first = at_row % 2 * cols
        block, at = k // groups, pl.ds(pl.multiple_of(k % groups * depth, depth), depth)
        cell_hot[block, :, at] = jnp.where(
            (cell == first + at_col) | (cell == first + ((at_col + 1) & (cols - 1))), 0.25, 0.0
        ).astype(jnp.bfloat16)
        pair = lax.shift_right_logical(at_row, 1)
        for p in range(rows // 2):
            hot = jnp.where(pair == p, 1.0, 0.0)
            row_hot[block, p, :, at] = jnp.broadcast_to(hot, (16, depth)).astype(jnp.bfloat16)
        return carry

    def deposit(c):
        start, size = chunks[c]
        at = pl.ds(start, size)
        tile = min(rows // 2, 2 ** (max(1, 1024 // size).bit_length() - 1))
        for block in range(n_lon // groups):
            def arrive(k, carry):
                await_group(k, lambda i: recv.at[i, at], recv_sem.at[c, k])
                return carry

            lax.fori_loop(block * groups, (block + 1) * groups, arrive, 0)
            first = block * groups * n_lat
            got = jnp.concatenate([recv[first + i, at, :] for i in range(groups * n_lat)], axis=1)
            stacked = got.reshape(size // 16, 16, wide)
            for t in range(rows // 2 // tile):
                lhs = []
                for j in range(tile):
                    lhs.append((stacked * row_hot[block, t * tile + j][None]).reshape(size, wide))
                found = nt_dot(jnp.concatenate(lhs, axis=0), cell_hot[block])
                for j in range(tile):
                    r = 2 * (t * tile + j)
                    here = found[j * size:(j + 1) * size]
                    low, high = here[:, 0:cols], here[:, cols:2 * cols]
                    if block > 0:
                        low, high = later[r, at, :] + low, later[r + 1, at, :] + high
                    later[r, at, :] = low
                    later[r + 1, at, :] = high

    assert 2 * rows <= cols and rows % 4 == 0
    half = jnp.bfloat16
    lane = lax.broadcasted_iota(jnp.int32, (PART, cols), 1)
    lane_half = lane.astype(jnp.float32).astype(half)
    side_half = jnp.where(lane == cols - 1, -0.5, 0.5)
    west, east = (lon + n_lon - 1) % n_lon, (lon + 1) % n_lon
    south, north = (lat + n_lat - 1) % n_lat, (lat + 1) % n_lat
    targets = ((lat, west), (lat, east), (south, lon), (north, lon))

    def edge_copy(step, c, side):
        at = pl.ds(*chunks[c])
        return pltpu.make_async_remote_copy(
            src_ref=edge_out.at[step, max(side, 1), at], dst_ref=edge_in.at[step, side, at],
            send_sem=edge_send_sem.at[step, c, side], recv_sem=edge_recv_sem.at[step, c, side],
            device_id=targets[side], device_id_type=MESH,
        )

    def send_edges(step, c):
        edge_copy(step, c, 0).start()
        edge_copy(step, c, 1).start()

        @pl.when(lat > 0)
        def _():
            edge_copy(step, c, 2).start()

        @pl.when(lat < n_lat - 1)
        def _():
            edge_copy(step, c, 3).start()

    def await_edges(step, c):
        edge_copy(step, c, 0).wait()
        edge_copy(step, c, 1).wait()

        @pl.when(lat > 0)
        def _():
            edge_copy(step, c, 2).wait_send()
            edge_copy(step, c, 3).wait_recv()

        @pl.when(lat < n_lat - 1)
        def _():
            edge_copy(step, c, 3).wait_send()
            edge_copy(step, c, 2).wait_recv()

    def split(s, w):
        flux = (0.5 * w) * s
        even = RATE * s
        return even + flux, even - flux

    def pack_row(packed, r, s, w):
        side = ((RATE + side_half * w) * s).astype(half)
        if r > 0:
            side = pltpu.roll(side, 2 * r, 1)
        here = (lane_half == half(2 * r)) | (lane_half == half((2 * r - 1) % cols))
        return jnp.where(here, side, packed)

    def pack_edge(step, at, r, s):
        if r == 0:
            edge_out[step, 2, at, :] = split(s, wlat[r, at, :])[0].astype(jnp.bfloat16)
        if r == rows - 1:
            edge_out[step, 3, at, :] = split(s, wlat[r, at, :])[1].astype(jnp.bfloat16)

    def parts(c, work):
        start, size = chunks[c]

        def some(q, carry):
            work(pl.ds(pl.multiple_of(start + q * PART, PART), PART))
            return carry

        lax.fori_loop(0, size // PART, some, 0)

    def combine(c):
        def work(at):
            packed = jnp.zeros((PART, cols), half)
            below = later[rows - 1, at, :]
            for r in range(rows):
                here = later[r, at, :]
                s = state[r, at, :] + (here + below)
                state[r, at, :] = s
                packed = pack_row(packed, r, s, wlon[r, at, :])
                pack_edge(0, at, r, s)
                below = here
            edge_out[0, 1, at, :] = packed

        parts(c, work)
        send_edges(0, c)

    def advance(step, c):
        last = step == STEPS - 1
        src = state if step % 2 == 0 else later
        dst = out if last else later if step % 2 == 0 else state

        def work(at):
            both = jnp.where(
                lane % 2 == 0,
                edge_in[step, 0, at, :].astype(jnp.float32),
                pltpu.roll(edge_in[step, 1, at, :].astype(jnp.float32), 2, 1),
            ).astype(half)
            packed = jnp.zeros((PART, cols), half)
            centre = None
            below = edge_in[step, 3, at, :].astype(jnp.float32)
            for r in range(rows + 1):
                if r < rows:
                    s = src[r, at, :]
                    plus, minus = split(s, wlon[r, at, :])
                    moved = pltpu.roll(both, (cols - 1 - 2 * r) % cols, 1)
                    moved = moved.astype(jnp.float32)
                    across = (
                        (1.0 - 4.0 * RATE) * s
                        + jnp.where(lane == cols - 1, moved, pltpu.roll(plus, cols - 1, 1))
                        + jnp.where(lane == 0, moved, pltpu.roll(minus, 1, 1))
                    )
                    above, here = split(s, wlat[r, at, :])
                else:
                    above = edge_in[step, 2, at, :].astype(jnp.float32)
                if r > 0:
                    total = centre + above
                    dst[r - 1, at, :] = total
                    if not last:
                        packed = pack_row(packed, r - 1, total, wlon[r - 1, at, :])
                        pack_edge(step + 1, at, r - 1, total)
                if r < rows:
                    centre = across + below
                    below = here
            if not last:
                edge_out[step + 1, 1, at, :] = packed

        await_edges(step, c)
        parts(c, work)
        if not last:
            send_edges(step + 1, c)

    n_chunks = len(chunks)
    for c in range(1, n_chunks):
        ship(c)
    lax.fori_loop(0, n_lon, read_meta, 0)
    for which, buf in enumerate((state, wlon, wlat)):
        pltpu.make_async_copy(buf, buf, load_sem.at[which]).wait()
    for c in range(n_chunks):
        deposit(c)
        combine(c)
    for step in range(STEPS):
        for c in range(n_chunks):
            advance(step, c)

    for c in range(len(chunks)):
        sent = send.at[pl.ds(0, n_dev - 1), pl.ds(*chunks[c])]
        pltpu.make_async_copy(sent, sent, send_sem.at[c]).wait()
    sent = meta_send.at[pl.ds(0, n_dev - 1)]
    pltpu.make_async_copy(sent, sent, meta_send_sem).wait()


def write_out(x, out, sem):
    def put(r, carry):
        pltpu.make_async_copy(x.at[r], out.at[:, r, :], sem).start()
        return carry

    lax.fori_loop(0, x.shape[0], put, 0)
    pltpu.make_async_copy(x, x, sem).wait()


def local(departures, footprint, channel_map, adjoint_in, wind_lon, wind_lat):
    n_lat, n_lon = lax.axis_size("lat"), lax.axis_size("lon")
    n_dev = n_lat * n_lon
    levels, rows, cols = adjoint_in.shape
    obs = departures.shape[0]
    capacity = 2 * obs // n_dev
    slots = -(-capacity // LANES) * LANES
    wide = min(n_dev * slots, max(4096, n_lat * slots))
    n_chunks = len(chunks_of(levels))
    block = pltpu.VMEM((n_dev, levels, slots), jnp.bfloat16)
    meta = pltpu.VMEM((n_dev, 1, slots), jnp.int32)
    field = pltpu.VMEM((rows, levels, cols), jnp.float32)
    edges = pltpu.VMEM((STEPS, 4, levels, cols), jnp.bfloat16)
    vmem, anywhere = pl.BlockSpec(memory_space=pltpu.VMEM), pl.BlockSpec(memory_space=pl.ANY)
    hbm = pl.BlockSpec(memory_space=pltpu.HBM)
    result = pl.pallas_call(
        functools.partial(kernel, n_lat, n_lon),
        out_shape=pltpu.VMEM((rows, levels, cols), jnp.float32),
        in_specs=[vmem, hbm, vmem] + [hbm] * 3,
        out_specs=vmem,
        scratch_shapes=[
            pltpu.VMEM(departures.shape, jnp.bfloat16),
            pltpu.VMEM((levels + META, obs), jnp.bfloat16),
            pltpu.VMEM((obs, slots), jnp.float32),
            block, block, meta, meta,
            pltpu.VMEM((n_dev * slots // wide, 2 * cols, wide), jnp.bfloat16),
            pltpu.VMEM((n_dev * slots // wide, rows // 2, 16, wide), jnp.bfloat16),
            field, field, field, field,
            edges, edges,
            pltpu.SemaphoreType.DMA((4,)),
            pltpu.SemaphoreType.DMA((n_chunks,)),
            pltpu.SemaphoreType.DMA((n_chunks, n_lon)),
            pltpu.SemaphoreType.DMA,
            pltpu.SemaphoreType.DMA((n_lon,)),
            pltpu.SemaphoreType.DMA((STEPS, n_chunks, 4)),
            pltpu.SemaphoreType.DMA((STEPS, n_chunks, 4)),
        ],
        compiler_params=pltpu.CompilerParams(
            collective_id=0, has_side_effects=True, vmem_limit_bytes=52 << 20
        ),
        name="assimilate",
    )(footprint.T, departures, channel_map, adjoint_in, wind_lon, wind_lat)
    return pl.pallas_call(
        write_out,
        out_shape=jax.ShapeDtypeStruct(adjoint_in.shape, jnp.float32),
        in_specs=[vmem],
        out_specs=hbm,
        scratch_shapes=[pltpu.SemaphoreType.DMA],
        compiler_params=pltpu.CompilerParams(vmem_limit_bytes=8 << 20),
        name="write_out",
    )(result)


def solution(mesh):
    in_specs = (
        P(("lat", "lon"), None),
        P(("lat", "lon"), None),
        P(),
        P(None, "lat", "lon"),
        P(None, "lat", "lon"),
        P(None, "lat", "lon"),
    )
    out_specs = P(None, "lat", "lon")
    return jax.shard_map(local, mesh=mesh, in_specs=in_specs, out_specs=out_specs, check_vma=False)
```
